512 devices in a mesh: dp: 8 (over x, core), expert: 64 (over y, z).
Axes of the slice: x: 4, y: 4, z: 16, core: 2. Of those that a mesh axis runs over, the one named last changes fastest.
Arguments:
- tokens: bfloat16 [65536, 2048], P(('dp', 'expert')), may hold values from -6 to 6
- out_grad: bfloat16 [65536, 2048], P(('dp', 'expert')), may hold values from -6 to 6
- route_gates: float32 [65536, 2], P(('dp', 'expert')), may hold values from 0.1 to 1
- route_slot: int32 [65536, 2], P(('dp', 'expert')), may hold values from 0 to 63, all different within a row; in each aligned block of 128 rows (0 to 127, 128 to 255, ...) at most 5 rows name the same one
- gate_weight: bfloat16 [64, 2048, 768], P('expert', 'dp'), may hold values from -0.125 to 0.125
- up_weight: bfloat16 [64, 2048, 768], P('expert', 'dp'), may hold values from -0.125 to 0.125
- down_weight: bfloat16 [64, 2048, 768], P('expert', 'dp'), may hold values from -0.21875 to 0.21875
Outputs:
- moe_out: bfloat16 [65536, 2048], P(('dp', 'expert'))
- token_grad: bfloat16 [65536, 2048], P(('dp', 'expert'))
- down_grad: bfloat16 [64, 2048, 768], P('expert', 'dp')
The draws below stay inside these ranges and needn't reach their ends.
Inputs may be any that keep to these rules, and one draw needn't show every extreme that they name: `route_slot`: the 2 routes of a token name different slots. At most 5 routes of the tokens of one device name one slot, and in every draw some device sends exactly 5 routes to some slot.
All inputs are finite; a program needn't handle non-finite values.
Results may differ from the reference program's by a relative error of at most 0.014.
Values may be sent and summed in bfloat16 or wider, within the bound.
A program may use at most 64 MiB of HBM per device.

```python
import math
import jax
import jax.numpy as jnp
import numpy as np
from jax import lax

D = 2048
FF = 768
TOPK = 2
TOK_DEV = 128
SLOTS = 64
CAP = 5
TOKENS = 65536
N_DP = 8
N_EXPERT = 64


def steps_of(rng, dims, pieces, least, largest):
    gain, own = 1.0, jax.random.fold_in(rng, 6)
    for dim, blocks in pieces:
        heights = jnp.exp(jax.random.uniform(jax.random.fold_in(own, dim), (blocks,), jnp.float32, least / len(pieces), largest / len(pieces)))
        gain = gain * jnp.repeat(heights, dims[dim] // blocks).reshape([-1 if axis == dim else 1 for axis in range(len(dims))])
    return gain


def deal_out(rng, own, number, rows, count, top, bound, skew):
    sequence = jax.random.permutation(rng, count)
    heavy_load, usual = shares(count, rows * top, bound, skew, True), shares(count, rows * top, bound, skew, False)
    places = jnp.arange(count)

    def named(lengths, offset_by):
        used = int((lengths > 0).sum())
        fixed = max(1, used // 4)
        shifted = fixed + (places - fixed + offset_by * (used - fixed)) % max(1, count - fixed)
        return jnp.zeros((count,), jnp.int32).at[sequence[jnp.where(places < fixed, places, shifted)]].set(jnp.asarray(lengths, jnp.int32))

    lengths = jnp.where(number % 4 == 0, named(heavy_load, number // 4), named(usual, number - number // 4 - 1))
    mixed = jax.random.permutation(jax.random.fold_in(own, 3), count)
    source_of, taker = mixed[0:count // 2 * 2:2], mixed[1:count // 2 * 2:2]
    slack = jnp.minimum(lengths[source_of] - 1, bound - lengths[taker]) // 2
    slack = jnp.where((source_of == sequence[0]) | (taker == sequence[0]) | (lengths[taker] == 0), 0, jnp.maximum(slack, 0))
    shifted = jax.random.randint(jax.random.fold_in(own, 4), (count // 2,), 0, 1 << 20) % (slack + 1)
    lengths = lengths.at[source_of].add(-shifted).at[taker].add(shifted)
    labels = jnp.searchsorted(jnp.cumsum(lengths), jnp.arange(rows * top), side="right").astype(jnp.int32)
    grid = labels.reshape(top, rows).T
    grid = grid[jax.random.permutation(jax.random.fold_in(own, 1), rows)]
    offset_by = jax.random.randint(jax.random.fold_in(own, 2), (rows, 1), 0, top)
    return jnp.take_along_axis(grid, (jnp.arange(top)[None, :] + offset_by) % top, axis=1)


def shares(number_of, total, bound, skew, full):
    weights = [(1 << 20) // math.isqrt(rank ** skew) + 1 for rank in range(1, number_of + 1)]
    largest = bound if full else min(bound, max(-(-total // number_of), total * weights[0] // sum(weights)))
    least = 1 if total - largest >= number_of - 1 else 0
    holding, spare = [largest] + [least] * (number_of - 1), total - largest - least * (number_of - 1)
    while spare > 0:
        candidates = [i for i in range(1, number_of) if holding[i] < largest] or [i for i in range(1, number_of) if holding[i] < bound]
        mass, budget = sum([weights[i] for i in candidates]), spare
        for i in candidates:
            extra = min(bound - holding[i], max(1, budget * weights[i] // mass), spare)
            holding[i] = holding[i] + extra
            spare = spare - extra
    return np.array(holding)


def normal_values(rng, shape, deviation, limit, cuts=(), held_as=jnp.bfloat16):
    result = deviation * jax.random.normal(rng, shape, jnp.float32)
    if cuts:
        result = result * steps_of(rng, shape, cuts, -0.22, 0.18)
    return jnp.clip(result, -limit, limit).astype(held_as)


def setup_inputs(seed: int = 0) -> dict:
    key_list = jax.random.split(jax.random.key(seed), 8)
    tokens = normal_values(key_list[0], (TOKENS, D), 1.0, 6.0, ((0, 512),))
    out_grad = normal_values(key_list[1], (TOKENS, D), 1.0, 6.0, ((0, 512),))
    route_gates = jnp.clip(0.1 + 0.9 * jax.random.uniform(key_list[2], (TOKENS, TOPK), jnp.float32) ** steps_of(key_list[2], (TOKENS, TOPK), ((0, 512),), -0.2, 0.2), 0.1, 1.0)
    route_slot_keys = jax.random.split(jax.random.fold_in(key_list[3], 1), TOKENS // TOK_DEV)
    route_slot_turns = jax.random.permutation(jax.random.fold_in(key_list[3], 3), TOKENS // TOK_DEV)
    route_slot = jax.vmap(lambda own, number: deal_out(jax.random.fold_in(key_list[3], 2), own, number, TOK_DEV, SLOTS, TOPK, CAP, 2))(route_slot_keys, route_slot_turns).reshape((TOKENS, TOPK))
    gate_weight = normal_values(key_list[4], (SLOTS, D, FF), D ** -0.5, 0.125, ((0, 64), (1, 8)))
    up_weight = normal_values(key_list[5], (SLOTS, D, FF), D ** -0.5, 0.125, ((0, 64), (1, 8)))
    down_weight = normal_values(key_list[6], (SLOTS, D, FF), FF ** -0.5, 0.21875, ((0, 64), (1, 8)))
    return dict(tokens=tokens, out_grad=out_grad, route_gates=route_gates, route_slot=route_slot, gate_weight=gate_weight, up_weight=up_weight, down_weight=down_weight)


def silu_parts(gate_proj):
    sigma_gate = jax.nn.sigmoid(gate_proj)
    return gate_proj * sigma_gate, sigma_gate


def reference(tokens, out_grad, route_gates, route_slot, gate_weight, up_weight, down_weight):
    route_total = TOK_DEV * TOPK
    buffer_rows = N_EXPERT * CAP
    all_routes = N_DP * N_EXPERT * route_total
    routes_dev = route_slot.reshape(N_DP, N_EXPERT, route_total).astype(jnp.int32)
    slot_ids = jnp.arange(SLOTS, dtype=jnp.int32)
    onehot = (routes_dev[:, :, :, None] == slot_ids[None, None, None, :]).astype(jnp.int32)
    slot_rank = jnp.sum((jnp.cumsum(onehot, axis=2) - onehot) * onehot, axis=3).astype(jnp.int32)
    group_index = jnp.broadcast_to(jnp.arange(N_DP, dtype=jnp.int32)[:, None, None], routes_dev.shape)
    source_index = jnp.broadcast_to(jnp.arange(N_EXPERT, dtype=jnp.int32)[None, :, None], routes_dev.shape)
    route_index = ((group_index * N_EXPERT + source_index) * route_total
                   + jnp.arange(route_total, dtype=jnp.int32)[None, None, :]).astype(jnp.int32)
    route_table = jnp.full((N_DP, SLOTS, buffer_rows), all_routes, jnp.int32)
    route_table = route_table.at[group_index, routes_dev, (source_index * CAP + slot_rank).astype(jnp.int32)].set(route_index)
    route_table = jnp.transpose(route_table, (1, 0, 2))
    gates_flat = route_gates.reshape(-1)

    def per_slot(totals, inputs):
        out_sum, grad_sum = totals
        index_rows, w_gate, w_up, w_down = inputs
        filled = index_rows < all_routes
        safe_index = jnp.where(filled, index_rows, 0).astype(jnp.int32)
        token_index = (safe_index // TOPK).astype(jnp.int32)
        gate_value = jnp.where(filled, gates_flat[safe_index], jnp.zeros((), gates_flat.dtype))
        rows_in = jnp.where(filled[:, :, None], tokens[token_index], jnp.zeros((), tokens.dtype)).reshape(-1, D)
        rows_grad = (gate_value[:, :, None] * out_grad[token_index].astype(jnp.float32)).astype(jnp.bfloat16).reshape(-1, D)
        gate_proj = jnp.dot(rows_in, w_gate, preferred_element_type=jnp.float32)
        up_proj = jnp.dot(rows_in, w_up, preferred_element_type=jnp.float32)
        activated, sigma_gate = silu_parts(gate_proj)
        hidden = (activated * up_proj).astype(jnp.bfloat16)
        outputs = jnp.dot(hidden, w_down.T, preferred_element_type=jnp.float32).astype(jnp.bfloat16)
        grad_hidden = jnp.dot(rows_grad, w_down, preferred_element_type=jnp.float32)
        grad_gate = (grad_hidden * up_proj * sigma_gate * (1.0 + gate_proj * (1.0 - sigma_gate))).astype(jnp.bfloat16)
        grad_up = (grad_hidden * activated).astype(jnp.bfloat16)
        grad_rows = (jnp.dot(grad_gate, w_gate.T, preferred_element_type=jnp.float32)
                     + jnp.dot(grad_up, w_up.T, preferred_element_type=jnp.float32)).astype(jnp.bfloat16)
        group_parts = jnp.einsum("grd,grf->gdf",
                                 rows_grad.reshape(N_DP, buffer_rows, D).astype(jnp.float32),
                                 hidden.reshape(N_DP, buffer_rows, FF).astype(jnp.float32)).astype(jnp.bfloat16)
        down_slot = jnp.sum(group_parts.astype(jnp.float32), axis=0).astype(jnp.bfloat16)
        target_rows = jnp.where(filled, token_index, TOKENS).reshape(-1).astype(jnp.int32)
        out_sum = out_sum.at[target_rows].add(gate_value.reshape(-1)[:, None] * outputs.astype(jnp.float32), mode="drop")
        grad_sum = grad_sum.at[target_rows].add(grad_rows.astype(jnp.float32), mode="drop")
        return (out_sum, grad_sum), down_slot

    start_sums = (jnp.zeros((TOKENS, D), jnp.float32), jnp.zeros((TOKENS, D), jnp.float32))
    (out_sum, grad_sum), down_grad = lax.scan(per_slot, start_sums, (route_table, gate_weight, up_weight, down_weight))
    return out_sum.astype(jnp.bfloat16), grad_sum.astype(jnp.bfloat16), down_grad
```

```python
import jax
import jax.numpy as jnp
from jax import lax
from jax.sharding import PartitionSpec as P

LANES = 128


def expert_forward(rows_in, w_gate, w_up, w_down):
    gate_proj = jnp.dot(rows_in, w_gate, preferred_element_type=jnp.float32)
    up_proj = jnp.dot(rows_in, w_up, preferred_element_type=jnp.float32)
    sigma_gate = jax.nn.sigmoid(gate_proj)
    activated = gate_proj * sigma_gate
    hidden = (activated * up_proj).astype(jnp.bfloat16)
    outputs = lax.dot_general(
        hidden, w_down, (((1,), (1,)), ((), ())), preferred_element_type=jnp.float32
    ).astype(jnp.bfloat16)
    return (outputs, gate_proj, up_proj, hidden)


def expert_backward(rows_grad, gate_proj, up_proj, w_gate, w_up, w_down):
    grad_hidden = jnp.dot(rows_grad, w_down, preferred_element_type=jnp.float32)
    sigma_gate = jax.nn.sigmoid(gate_proj)
    activated = gate_proj * sigma_gate
    grad_gate = (
        grad_hidden * up_proj * sigma_gate * (1.0 + gate_proj * (1.0 - sigma_gate))
    ).astype(jnp.bfloat16)
    grad_up = (grad_hidden * activated).astype(jnp.bfloat16)
    contract_dims = (((1,), (1,)), ((), ()))
    summed = lax.dot_general(
        grad_gate, w_gate, contract_dims, preferred_element_type=jnp.float32
    ) + lax.dot_general(grad_up, w_up, contract_dims, preferred_element_type=jnp.float32)
    return summed.astype(jnp.bfloat16)


def per_device(tokens, out_grad, route_gates, route_slot, gate_weight, up_weight, down_weight):
    tok_dev, model_width = tokens.shape
    route_count = route_slot.shape[1]
    peer_count = lax.axis_size("expert")
    capacity = max(2, (5 * tok_dev * route_count + 4 * peer_count - 1) // (4 * peer_count))
    route_total = tok_dev * route_count
    send_rows = peer_count * capacity
    flat_slot = route_slot.reshape(-1)
    onehot = (flat_slot[:, None] == jnp.arange(peer_count, dtype=jnp.int32)[None, :]).astype(
        jnp.int32
    )
    slot_rank = jnp.sum((jnp.cumsum(onehot, axis=0) - onehot) * onehot, axis=1)
    send_index = flat_slot * capacity + slot_rank
    route_of_row = (
        jnp.full((send_rows,), route_total, jnp.int32)
        .at[send_index]
        .set(jnp.arange(route_total, dtype=jnp.int32))
    )
    filled = route_of_row < route_total
    safe_route = jnp.where(filled, route_of_row, 0)
    token_row = safe_route // route_count
    gate_value = jnp.where(filled, route_gates.reshape(-1)[safe_route], 0.0)
    tile = (model_width // LANES, LANES)
    token_tiles = tokens.reshape(tok_dev, *tile)
    grad_tiles = out_grad.reshape(tok_dev, *tile)
    rows_in = jnp.where(filled[:, None, None], token_tiles[token_row], jnp.zeros((), tokens.dtype))
    rows_in = rows_in.reshape(peer_count, capacity * tile[0], LANES)
    rows_grad = (
        gate_value[:, None, None] * grad_tiles[token_row].astype(jnp.float32)
    ).astype(jnp.bfloat16)
    rows_grad = rows_grad.reshape(peer_count, capacity * tile[0], LANES)
    full_gate, full_up, full_down = (
        lax.all_gather(gate_weight, "dp", axis=1, tiled=True),
        lax.all_gather(up_weight, "dp", axis=1, tiled=True),
        lax.all_gather(down_weight, "dp", axis=1, tiled=True),
    )
    w_gate = full_gate[0]
    w_up = full_up[0]
    w_down = full_down[0]
    item_shape = (peer_count, capacity * tile[0], LANES)
    received = lax.all_to_all(rows_in, "expert", split_axis=0, concat_axis=0, tiled=True)
    outputs, gate_proj, up_proj, hidden_saved = expert_forward(
        received.reshape(-1, model_width), w_gate, w_up, w_down
    )
    out_back = lax.all_to_all(
        outputs.reshape(item_shape), "expert", split_axis=0, concat_axis=0, tiled=True
    )
    grad_in = lax.all_to_all(rows_grad, "expert", split_axis=0, concat_axis=0, tiled=True)
    grad_rows = expert_backward(
        grad_in.reshape(-1, model_width), gate_proj, up_proj, w_gate, w_up, w_down
    )
    grad_back = lax.all_to_all(
        grad_rows.reshape(item_shape), "expert", split_axis=0, concat_axis=0, tiled=True
    )
    grad_flat = grad_in.reshape(-1, model_width)
    down_share = lax.psum_scatter(
        lax.dot_general(
            grad_flat, hidden_saved, (((0,), (0,)), ((), ())), preferred_element_type=jnp.float32
        ).astype(jnp.bfloat16),
        "dp",
        scatter_dimension=0,
        tiled=True,
    )
    down_grad = down_share[None]
    out_routes = out_back.reshape(send_rows, *tile)[send_index].astype(jnp.float32)
    out_routes = out_routes.reshape(tok_dev, route_count, *tile)
    moe_out = jnp.sum(route_gates[:, :, None, None] * out_routes, axis=1).astype(jnp.bfloat16)
    moe_out = moe_out.reshape(tok_dev, model_width)
    grad_routes = grad_back.reshape(send_rows, *tile)[send_index].astype(jnp.float32)
    token_grad = jnp.sum(grad_routes.reshape(tok_dev, route_count, *tile), axis=1).astype(
        jnp.bfloat16
    )
    token_grad = token_grad.reshape(tok_dev, model_width)
    return (moe_out, token_grad, down_grad)


def solution(mesh):
    placed = (
        P(("dp", "expert"), None),
        P(("dp", "expert"), None),
        P(("dp", "expert"), None),
        P(("dp", "expert"), None),
        P("expert", "dp", None),
        P("expert", "dp", None),
        P("expert", "dp", None),
    )
    return jax.shard_map(
        per_device,
        mesh=mesh,
        in_specs=placed,
        out_specs=(P(("dp", "expert"), None), P(("dp", "expert"), None), P("expert", "dp", None)),
        check_vma=False,
    )
```

```python
import functools

import jax
import jax.numpy as jnp
from jax import lax
from jax.experimental import pallas as pl
from jax.experimental.pallas import tpu as pltpu
from jax.sharding import PartitionSpec as P

LANES = 128
SUB = 16
NX, NY, NZ = 4, 4, 16
BACK = NZ - 1
WIDE = 256
MESH = pl.DeviceIdType.MESH
X, DY, Y, DX = range(4)


def layer(
    cap,
    row_of_ref,
    gate_of_ref,
    row_of_col_ref,
    gate_of_col_ref,
    tokens_ref,
    grads_ref,
    gate_in,
    up_in,
    down_in,
    moe_ref,
    tgrad_ref,
    dgrad_ref,
    perm,
    w_gate,
    w_up,
    w_down,
    sent,
    got,
    relay,
    rows_x,
    rows_dy,
    rows_tmp,
    slope,
    act,
    hidden,
    d_gate,
    d_up,
    part,
    parts,
    send_sem,
    recv_sem,
    relay_sem,
    pass_sem,
    own_sem,
    w_own,
    w_send,
    w_pass,
    w_recv,
    p_send,
    p_recv,
):
    f32, bf16 = jnp.float32, jnp.bfloat16
    dp, e = lax.axis_index("dp"), lax.axis_index("expert")
    y, z = e // NZ, e % NZ
    chip, core = dp // 2, dp % 2
    n_exp, n_dp = NY * NZ, NX * 2
    rows = n_exp * cap
    width = tokens_ref.shape[1]
    shard = width // n_dp
    ff = hidden.shape[1]
    unit = cap * SUB

    barrier = pltpu.get_barrier_semaphore()

    def greet(k, _):
        pl.semaphore_signal(
            barrier, inc=1, device_id=(dp, (e + k) % n_exp), device_id_type=MESH
        )
        return 0

    lax.fori_loop(1, n_exp, greet, 0)
    for k in range(1, n_dp):
        pl.semaphore_signal(barrier, inc=1, device_id=((dp + k) % n_dp, e), device_id_type=MESH)

    def block(p):
        return pl.ds(pl.multiple_of(p * unit, SUB), unit)

    def owner_rows(p):
        return pl.ds(pl.multiple_of(p * shard, shard), shard)

    def cols(n):
        return pl.ds(pl.multiple_of(n * WIDE, WIDE), WIDE)

    at = lax.broadcasted_iota(jnp.int32, (WIDE, WIDE), 0)
    to = lax.broadcasted_iota(jnp.int32, (WIDE, WIDE), 1)
    perm[...] = jnp.where((at % SUB) * SUB + at // SUB == to, 1.0, 0.0).astype(bf16)

    def to_tiles(nat, flat):
        def step(g, _):
            halves = []
            for h in range(2):
                r = pl.ds(pl.multiple_of(g * 32 + h * SUB, SUB), SUB)
                halves.append(
                    jnp.concatenate(
                        [nat[r, j * LANES : (j + 1) * LANES] for j in range(SUB)], axis=0
                    )
                )
            moved = jnp.dot(
                perm[...], jnp.concatenate(halves, axis=1), preferred_element_type=f32
            ).astype(bf16)
            for h in range(2):
                r = pl.ds(pl.multiple_of(g * 512 + h * WIDE, WIDE), WIDE)
                flat[r, :] = moved[:, h * LANES : (h + 1) * LANES]
            return 0

        lax.fori_loop(0, rows // 32, step, 0)

    def to_rows(flat, nat):
        def step(g, _):
            halves = [
                flat[pl.ds(pl.multiple_of(g * 512 + h * WIDE, WIDE), WIDE), :] for h in range(2)
            ]
            moved = jnp.dot(
                perm[...], jnp.concatenate(halves, axis=1), preferred_element_type=f32
            ).astype(bf16)
            for h in range(2):
                r = pl.ds(pl.multiple_of(g * 32 + h * SUB, SUB), SUB)
                for j in range(SUB):
                    nat[r, j * LANES : (j + 1) * LANES] = moved[
                        j * SUB : (j + 1) * SUB, h * LANES : (h + 1) * LANES
                    ]
            return 0

        lax.fori_loop(0, rows // 32, step, 0)

    def send(ph, p):
        pltpu.make_async_remote_copy(
            sent.at[ph, block(p)],
            got.at[ph, block(e)],
            send_sem.at[ph],
            recv_sem.at[ph],
            device_id=(dp, p),
            device_id_type=MESH,
        ).start()

    def exchange(ph):
        far = (z + NZ // 2) % NZ
        for a in (2, 3):
            pltpu.make_async_remote_copy(
                sent.at[ph, block((y + a) % NY * NZ + far)],
                relay.at[ph, pl.ds((a - 2) * unit, unit)],
                send_sem.at[ph],
                relay_sem.at[ph],
                device_id=(dp, y * NZ + (z + BACK) % NZ),
                device_id_type=MESH,
            ).start()
        pltpu.make_async_copy(
            sent.at[ph, block(e)], got.at[ph, block(e)], own_sem.at[ph]
        ).start()
        for a in (0, 1):
            send(ph, (y + a) % NY * NZ + far)

        def step(i, _):
            for a in range(NY):
                send(ph, (y + a) % NY * NZ + (z + i) % NZ)
                send(ph, (y + a) % NY * NZ + (z + NZ // 2 + i) % NZ)
            return 0

        lax.fori_loop(1, NZ // 2, step, 0)
        for a in range(1, NY):
            send(ph, (y + a) % NY * NZ + z)

    def pass_on(ph):
        came = (z + NZ - BACK) % NZ
        pltpu.make_async_remote_copy(
            relay.at[ph],
            relay.at[ph],
            pass_sem.at[ph],
            relay_sem.at[ph],
            device_id=(dp, y * NZ + came),
            device_id_type=MESH,
        ).wait_recv()
        for a in (2, 3):
            pltpu.make_async_remote_copy(
                relay.at[ph, pl.ds((a - 2) * unit, unit)],
                got.at[ph, block(y * NZ + came)],
                pass_sem.at[ph],
                recv_sem.at[ph],
                device_id=(dp, (y + a) % NY * NZ + (came + NZ // 2) % NZ),
                device_id_type=MESH,
            ).start()

    next_e = y * NZ + (z + 1) % NZ

    def arrived(ph):
        most = pl.ds(0, (n_exp - 1) * unit)
        pltpu.make_async_remote_copy(
            sent.at[ph, most],
            got.at[ph, most],
            send_sem.at[ph],
            recv_sem.at[ph],
            device_id=(dp, next_e),
            device_id_type=MESH,
        ).wait_recv()
        pltpu.make_async_copy(
            sent.at[ph, block(e)], got.at[ph, block(e)], own_sem.at[ph]
        ).wait()

    def drained(ph):
        most = pl.ds(0, (n_exp - 1) * unit)
        pltpu.make_async_remote_copy(
            sent.at[ph, most],
            got.at[ph, most],
            send_sem.at[ph],
            recv_sem.at[ph],
            device_id=(dp, next_e),
            device_id_type=MESH,
        ).wait_send()
        pltpu.make_async_remote_copy(
            relay.at[ph],
            relay.at[ph],
            pass_sem.at[ph],
            relay_sem.at[ph],
            device_id=(dp, next_e),
            device_id_type=MESH,
        ).wait_send()

    slot_row = lax.broadcasted_iota(jnp.int32, (rows, tokens_ref.shape[0]), 0)
    hit0 = slot_row == row_of_ref[0:1, :]
    hit1 = slot_row == row_of_ref[1:2, :]
    pick = jnp.where(hit0 | hit1, 1.0, 0.0).astype(bf16)

    def gather_x(n, _):
        rows_tmp[:, cols(n)] = jnp.dot(
            pick, tokens_ref[:, cols(n)], preferred_element_type=f32
        ).astype(bf16)
        return 0

    lax.fori_loop(0, width // WIDE, gather_x, 0)
    to_tiles(rows_tmp, sent.at[X])

    pl.semaphore_wait(barrier, n_exp - 1 + n_dp - 1)

    turn = 1 - 2 * core
    partner = chip * 2 + 1 - core
    ahead = (chip + NX + turn) % NX * 2 + core
    behind = (chip + NX - turn) % NX * 2 + core
    across = (chip + 2) % NX * 2 + core
    stages = ((0, gate_in, w_gate), (1, up_in, w_up), (2, down_in, w_down))
    for kind, src, full in stages:
        pltpu.make_async_copy(src, full.at[owner_rows(dp)], w_own.at[kind]).start()
        for peer in (ahead, behind, partner):
            pltpu.make_async_remote_copy(
                src,
                full.at[owner_rows(dp)],
                w_send.at[kind],
                w_recv.at[kind, dp],
                device_id=(peer, e),
                device_id_type=MESH,
            ).start()

    exchange(X)
    pass_on(X)

    def weight_in(kind, full, owner):
        pltpu.make_async_remote_copy(
            full.at[owner_rows(owner)],
            full.at[owner_rows(owner)],
            w_pass.at[kind],
            w_recv.at[kind, owner],
            device_id=(partner, e),
            device_id_type=MESH,
        ).wait_recv()

    def weight_on(kind, full, owner, peer):
        pltpu.make_async_remote_copy(
            full.at[owner_rows(owner)],
            full.at[owner_rows(owner)],
            w_pass.at[kind],
            w_recv.at[kind, owner],
            device_id=(peer, e),
            device_id_type=MESH,
        ).start()

    for kind, _, full in stages:
        weight_in(kind, full, behind)
        weight_on(kind, full, behind, ahead)
        weight_on(kind, full, behind, partner)
        weight_in(kind, full, ahead)
        weight_on(kind, full, ahead, partner)

    share = jnp.sum(
        jnp.where(hit0, gate_of_ref[0:1, :], 0.0) + jnp.where(hit1, gate_of_ref[1:2, :], 0.0),
        axis=1,
        keepdims=True,
    )

    def gather_dy(n, _):
        taken = jnp.dot(pick, grads_ref[:, cols(n)], preferred_element_type=f32)
        rows_tmp[:, cols(n)] = (share * taken).astype(bf16)
        return 0

    lax.fori_loop(0, width // WIDE, gather_dy, 0)
    to_tiles(rows_tmp, sent.at[DY])
    exchange(DY)

    for kind, _, full in stages:
        weight_in(kind, full, across)
        weight_on(kind, full, across, partner)
    for kind, src, full in stages:
        pltpu.make_async_copy(src, full.at[owner_rows(dp)], w_own.at[kind]).wait()
        for k in range(NX):
            weight_in(kind, full, (chip + k) % NX * 2 + 1 - core)

    arrived(X)
    to_rows(got.at[X], rows_x)

    def forward(n, _):
        gate = jnp.dot(rows_x[...], w_gate[:, cols(n)], preferred_element_type=f32)
        up = jnp.dot(rows_x[...], w_up[:, cols(n)], preferred_element_type=f32)
        sigma = jax.nn.sigmoid(gate)
        activated = gate * sigma
        act[:, cols(n)] = activated
        slope[:, cols(n)] = up * sigma * (1.0 + gate * (1.0 - sigma))
        hidden[:, cols(n)] = (activated * up).astype(bf16)
        return 0

    lax.fori_loop(0, ff // WIDE, forward, 0)
    across_ff = (((1,), (1,)), ((), ()))

    def project(n, _):
        rows_tmp[:, cols(n)] = lax.dot_general(
            hidden[...], w_down[cols(n), :], across_ff, preferred_element_type=f32
        ).astype(bf16)
        return 0

    lax.fori_loop(0, width // WIDE, project, 0)
    to_tiles(rows_tmp, sent.at[Y])
    pass_on(DY)
    exchange(Y)

    arrived(DY)
    to_rows(got.at[DY], rows_dy)

    def backward(n, _):
        d_hidden = jnp.dot(rows_dy[...], w_down[:, cols(n)], preferred_element_type=f32)
        d_gate[:, cols(n)] = (d_hidden * slope[:, cols(n)]).astype(bf16)
        d_up[:, cols(n)] = (d_hidden * act[:, cols(n)]).astype(bf16)
        return 0

    lax.fori_loop(0, ff // WIDE, backward, 0)

    def project_back(n, _):
        rows_tmp[:, cols(n)] = (
            lax.dot_general(d_gate[...], w_gate[cols(n), :], across_ff, preferred_element_type=f32)
            + lax.dot_general(d_up[...], w_up[cols(n), :], across_ff, preferred_element_type=f32)
        ).astype(bf16)
        return 0

    lax.fori_loop(0, width // WIDE, project_back, 0)
    to_tiles(rows_tmp, sent.at[DX])
    pass_on(Y)
    exchange(DX)

    def outer(n, _):
        part[cols(n), :] = lax.dot_general(
            rows_dy[:, cols(n)], hidden[...], (((0,), (0,)), ((), ())), preferred_element_type=f32
        ).astype(bf16)
        return 0

    lax.fori_loop(0, width // WIDE, outer, 0)
    pltpu.make_async_copy(part.at[owner_rows(dp)], parts.at[owner_rows(dp)], own_sem.at[4]).start()
    for k in range(1, n_dp):
        peer = (dp + k) % n_dp
        pltpu.make_async_remote_copy(
            part.at[owner_rows(peer)],
            parts.at[owner_rows(dp)],
            p_send,
            p_recv,
            device_id=(peer, e),
            device_id_type=MESH,
        ).start()

    token_col = lax.broadcasted_iota(jnp.int32, (tokens_ref.shape[0], rows), 1)
    home0 = jnp.where(token_col == row_of_col_ref[:, 0:1], 1.0, 0.0).astype(bf16)
    home1 = jnp.where(token_col == row_of_col_ref[:, 1:2], 1.0, 0.0).astype(bf16)

    arrived(Y)
    to_rows(got.at[Y], rows_tmp)

    def combine(n, _):
        first = jnp.dot(home0, rows_tmp[:, cols(n)], preferred_element_type=f32)
        second = jnp.dot(home1, rows_tmp[:, cols(n)], preferred_element_type=f32)
        moe_ref[:, cols(n)] = (
            gate_of_col_ref[:, 0:1] * first + gate_of_col_ref[:, 1:2] * second
        ).astype(bf16)
        return 0

    lax.fori_loop(0, width // WIDE, combine, 0)
    pass_on(DX)

    others = pl.ds(0, (n_dp - 1) * shard)
    pltpu.make_async_remote_copy(
        part.at[others], parts.at[others], p_send, p_recv, device_id=(partner, e), device_id_type=MESH
    ).wait_recv()
    pltpu.make_async_copy(part.at[owner_rows(dp)], parts.at[owner_rows(dp)], own_sem.at[4]).wait()

    def total(n, _):
        acc = None
        for p in range(n_dp):
            r = pl.ds(pl.multiple_of(p * shard + n * 32, 32), 32)
            term = parts[r, :].astype(f32)
            acc = term if acc is None else acc + term
        dgrad_ref[pl.ds(pl.multiple_of(n * 32, 32), 32), :] = acc.astype(bf16)
        return 0

    lax.fori_loop(0, shard // 32, total, 0)

    arrived(DX)
    to_rows(got.at[DX], rows_tmp)
    home = home0 + home1

    def collect(n, _):
        tgrad_ref[:, cols(n)] = jnp.dot(
            home, rows_tmp[:, cols(n)], preferred_element_type=f32
        ).astype(bf16)
        return 0

    lax.fori_loop(0, width // WIDE, collect, 0)

    for ph in range(4):
        drained(ph)
    for kind, src, full in stages:
        own3, on4 = pl.ds(0, 3 * shard), pl.ds(0, 4 * shard)
        pltpu.make_async_remote_copy(
            full.at[own3], full.at[own3], w_send.at[kind], w_recv.at[kind, dp],
            device_id=(partner, e), device_id_type=MESH,
        ).wait_send()
        pltpu.make_async_remote_copy(
            full.at[on4], full.at[on4], w_pass.at[kind], w_recv.at[kind, dp],
            device_id=(partner, e), device_id_type=MESH,
        ).wait_send()
    pltpu.make_async_remote_copy(
        part.at[others], parts.at[others], p_send, p_recv, device_id=(partner, e), device_id_type=MESH
    ).wait_send()


def per_device(tokens, out_grad, route_gates, route_slot, gate_weight, up_weight, down_weight):
    tok_dev, width = tokens.shape
    top = route_slot.shape[1]
    n_exp = lax.axis_size("expert")
    n_dp = lax.axis_size("dp")
    cap = max(2, (5 * tok_dev * top + 4 * n_exp - 1) // (4 * n_exp))
    rows = n_exp * cap
    ff = gate_weight.shape[2]
    shard = width // n_dp
    slots = route_slot.reshape(-1)
    order = jnp.arange(slots.shape[0], dtype=jnp.int32)
    earlier = (slots[:, None] == slots[None, :]) & (order[None, :] < order[:, None])
    row_of = slots * cap + jnp.sum(earlier.astype(jnp.int32), axis=1)
    row_of = row_of.reshape(tok_dev, top)

    bf16, f32 = jnp.bfloat16, jnp.float32
    vmem = pl.BlockSpec(memory_space=pltpu.VMEM)
    away = pl.BlockSpec(memory_space=pl.ANY)
    dma = pltpu.SemaphoreType.DMA
    flat = rows * SUB
    moe, tgrad, dgrad = pl.pallas_call(
        functools.partial(layer, cap),
        out_shape=(
            jax.ShapeDtypeStruct((tok_dev, width), bf16),
            jax.ShapeDtypeStruct((tok_dev, width), bf16),
            jax.ShapeDtypeStruct((shard, ff), bf16),
        ),
        in_specs=[vmem] * 6 + [away] * 3,
        out_specs=(vmem, vmem, vmem),
        scratch_shapes=[
            pltpu.VMEM((WIDE, WIDE), bf16),
            pltpu.VMEM((width, ff), bf16),
            pltpu.VMEM((width, ff), bf16),
            pltpu.VMEM((width, ff), bf16),
            pltpu.VMEM((4, flat, LANES), bf16),
            pltpu.VMEM((4, flat, LANES), bf16),
            pltpu.VMEM((4, 2 * cap * SUB, LANES), bf16),
            pltpu.VMEM((rows, width), bf16),
            pltpu.VMEM((rows, width), bf16),
            pltpu.VMEM((rows, width), bf16),
            pltpu.VMEM((rows, ff), f32),
            pltpu.VMEM((rows, ff), f32),
            pltpu.VMEM((rows, ff), bf16),
            pltpu.VMEM((rows, ff), bf16),
            pltpu.VMEM((rows, ff), bf16),
            pltpu.VMEM((width, ff), bf16),
            pltpu.VMEM((width, ff), bf16),
            dma((4,)),
            dma((4,)),
            dma((4,)),
            dma((4,)),
            dma((5,)),
            dma((3,)),
            dma((3,)),
            dma((3,)),
            dma((3, n_dp)),
            dma,
            dma,
        ],
        name="expert_layer",
        compiler_params=pltpu.CompilerParams(
            collective_id=0, has_side_effects=True, vmem_limit_bytes=60 * 1024 * 1024
        ),
    )(
        row_of.T,
        route_gates.T,
        row_of,
        route_gates,
        tokens,
        out_grad,
        gate_weight[0],
        up_weight[0],
        down_weight[0],
    )
    return moe, tgrad, dgrad[None]


def solution(mesh):
    rows = P(("dp", "expert"), None)
    weights = P("expert", "dp", None)
    return jax.shard_map(
        per_device,
        mesh=mesh,
        in_specs=(rows, rows, rows, rows, weights, weights, weights),
        out_specs=(rows, rows, weights),
        check_vma=False,
    )
```

```python
import functools

import jax
import jax.numpy as jnp
from jax import lax
from jax.experimental import pallas as pl
from jax.experimental.pallas import tpu as pltpu
from jax.sharding import PartitionSpec as P

LANES = 128
SUB = 16
NX, NY, NZ = 4, 4, 16
WIDE = 256
MESH = pl.DeviceIdType.MESH
X, DY, Y, DX = range(4)


def layer(
    cap,
    row_of_ref,
    gate_of_ref,
    row_of_col_ref,
    gate_of_col_ref,
    tokens_ref,
    grads_ref,
    gate_in,
    up_in,
    down_in,
    moe_ref,
    tgrad_ref,
    dgrad_ref,
    perm,
    w_gate,
    w_up,
    w_down,
    sent,
    got,
    rows_x,
    rows_dy,
    rows_tmp,
    slope,
    act,
    hidden,
    d_gate,
    d_up,
    part,
    parts,
    send_sem,
    recv_sem,
    own_sem,
    w_own,
    w_send,
    w_pass,
    w_recv,
    p_send,
    p_recv,
):
    f32, bf16 = jnp.float32, jnp.bfloat16
    dp, e = lax.axis_index("dp"), lax.axis_index("expert")
    y, z = e // NZ, e % NZ
    chip, core = dp // 2, dp % 2
    n_exp, n_dp = NY * NZ, NX * 2
    rows = n_exp * cap
    width = tokens_ref.shape[1]
    shard = width // n_dp
    ff = hidden.shape[1]
    unit = cap * SUB

    barrier = pltpu.get_barrier_semaphore()

    def greet(k, _):
        pl.semaphore_signal(
            barrier, inc=1, device_id=(dp, (e + k) % n_exp), device_id_type=MESH
        )
        return 0

    lax.fori_loop(1, n_exp, greet, 0)
    for k in range(1, n_dp):
        pl.semaphore_signal(barrier, inc=1, device_id=((dp + k) % n_dp, e), device_id_type=MESH)

    def block(p):
        return pl.ds(pl.multiple_of(p * unit, SUB), unit)

    def owner_rows(p):
        return pl.ds(pl.multiple_of(p * shard, shard), shard)

    def cols(n):
        return pl.ds(pl.multiple_of(n * WIDE, WIDE), WIDE)

    at = lax.broadcasted_iota(jnp.int32, (WIDE, WIDE), 0)
    to = lax.broadcasted_iota(jnp.int32, (WIDE, WIDE), 1)
    perm[...] = jnp.where((at % SUB) * SUB + at // SUB == to, 1.0, 0.0).astype(bf16)

    def to_tiles(nat, flat):
        def step(g, _):
            halves = []
            for h in range(2):
                r = pl.ds(pl.multiple_of(g * 32 + h * SUB, SUB), SUB)
                halves.append(
                    jnp.concatenate(
                        [nat[r, j * LANES : (j + 1) * LANES] for j in range(SUB)], axis=0
                    )
                )
            moved = jnp.dot(
                perm[...], jnp.concatenate(halves, axis=1), preferred_element_type=f32
            ).astype(bf16)
            for h in range(2):
                r = pl.ds(pl.multiple_of(g * 512 + h * WIDE, WIDE), WIDE)
                flat[r, :] = moved[:, h * LANES : (h + 1) * LANES]
            return 0

        lax.fori_loop(0, rows // 32, step, 0)

    def to_rows(flat, nat):
        def step(g, _):
            halves = [
                flat[pl.ds(pl.multiple_of(g * 512 + h * WIDE, WIDE), WIDE), :] for h in range(2)
            ]
            moved = jnp.dot(
                perm[...], jnp.concatenate(halves, axis=1), preferred_element_type=f32
            ).astype(bf16)
            for h in range(2):
                r = pl.ds(pl.multiple_of(g * 32 + h * SUB, SUB), SUB)
                for j in range(SUB):
                    nat[r, j * LANES : (j + 1) * LANES] = moved[
                        j * SUB : (j + 1) * SUB, h * LANES : (h + 1) * LANES
                    ]
            return 0

        lax.fori_loop(0, rows // 32, step, 0)

    def send(ph, p):
        pltpu.make_async_remote_copy(
            sent.at[ph, block(p)],
            got.at[ph, block(e)],
            send_sem.at[ph],
            recv_sem.at[ph],
            device_id=(dp, p),
            device_id_type=MESH,
        ).start()

    def exchange(ph):
        pltpu.make_async_copy(
            sent.at[ph, block(e)], got.at[ph, block(e)], own_sem.at[ph]
        ).start()
        for a in range(1, NY):
            send(ph, (y + a) % NY * NZ + z)

        def step(i, _):
            for a in range(NY):
                send(ph, (y + a) % NY * NZ + (z + i) % NZ)
            return 0

        lax.fori_loop(1, NZ, step, 0)

    next_e = y * NZ + (z + 1) % NZ

    def arrived(ph):
        most = pl.ds(0, (n_exp - 1) * unit)
        pltpu.make_async_remote_copy(
            sent.at[ph, most],
            got.at[ph, most],
            send_sem.at[ph],
            recv_sem.at[ph],
            device_id=(dp, next_e),
            device_id_type=MESH,
        ).wait_recv()
        pltpu.make_async_copy(
            sent.at[ph, block(e)], got.at[ph, block(e)], own_sem.at[ph]
        ).wait()

    def drained(ph):
        most = pl.ds(0, (n_exp - 1) * unit)
        pltpu.make_async_remote_copy(
            sent.at[ph, most],
            got.at[ph, most],
            send_sem.at[ph],
            recv_sem.at[ph],
            device_id=(dp, next_e),
            device_id_type=MESH,
        ).wait_send()

    slot_row = lax.broadcasted_iota(jnp.int32, (rows, tokens_ref.shape[0]), 0)
    hit0 = slot_row == row_of_ref[0:1, :]
    hit1 = slot_row == row_of_ref[1:2, :]
    pick = jnp.where(hit0 | hit1, 1.0, 0.0).astype(bf16)

    def gather_x(n, _):
        rows_tmp[:, cols(n)] = jnp.dot(
            pick, tokens_ref[:, cols(n)], preferred_element_type=f32
        ).astype(bf16)
        return 0

    lax.fori_loop(0, width // WIDE, gather_x, 0)
    to_tiles(rows_tmp, sent.at[X])

    pl.semaphore_wait(barrier, n_exp - 1 + n_dp - 1)

    turn = 1 - 2 * core
    partner = chip * 2 + 1 - core
    ahead = (chip + NX + turn) % NX * 2 + core
    behind = (chip + NX - turn) % NX * 2 + core
    across = (chip + 2) % NX * 2 + core
    stages = ((0, gate_in, w_gate), (1, up_in, w_up), (2, down_in, w_down))
    for kind, src, full in stages:
        pltpu.make_async_copy(src, full.at[owner_rows(dp)], w_own.at[kind]).start()
        for peer in (ahead, behind, partner):
            pltpu.make_async_remote_copy(
                src,
                full.at[owner_rows(dp)],
                w_send.at[kind],
                w_recv.at[kind, dp],
                device_id=(peer, e),
                device_id_type=MESH,
            ).start()

    exchange(X)

    def weight_in(kind, full, owner):
        pltpu.make_async_remote_copy(
            full.at[owner_rows(owner)],
            full.at[owner_rows(owner)],
            w_pass.at[kind],
            w_recv.at[kind, owner],
            device_id=(partner, e),
            device_id_type=MESH,
        ).wait_recv()

    def weight_on(kind, full, owner, peer):
        pltpu.make_async_remote_copy(
            full.at[owner_rows(owner)],
            full.at[owner_rows(owner)],
            w_pass.at[kind],
            w_recv.at[kind, owner],
            device_id=(peer, e),
            device_id_type=MESH,
        ).start()

    share = jnp.sum(
        jnp.where(hit0, gate_of_ref[0:1, :], 0.0) + jnp.where(hit1, gate_of_ref[1:2, :], 0.0),
        axis=1,
        keepdims=True,
    )

    def gather_dy(n, _):
        taken = jnp.dot(pick, grads_ref[:, cols(n)], preferred_element_type=f32)
        rows_tmp[:, cols(n)] = (share * taken).astype(bf16)
        return 0

    lax.fori_loop(0, width // WIDE, gather_dy, 0)
    to_tiles(rows_tmp, sent.at[DY])
    exchange(DY)

    for kind, _, full in stages:
        weight_in(kind, full, behind)
        weight_on(kind, full, behind, ahead)
        weight_on(kind, full, behind, partner)
        weight_in(kind, full, ahead)
        weight_on(kind, full, ahead, partner)

    for kind, _, full in stages:
        weight_in(kind, full, across)
        weight_on(kind, full, across, partner)
    for kind, src, full in stages:
        pltpu.make_async_copy(src, full.at[owner_rows(dp)], w_own.at[kind]).wait()
        for k in range(NX):
            weight_in(kind, full, (chip + k) % NX * 2 + 1 - core)

    arrived(X)
    to_rows(got.at[X], rows_x)

    def forward(n, _):
        gate = jnp.dot(rows_x[...], w_gate[:, cols(n)], preferred_element_type=f32)
        up = jnp.dot(rows_x[...], w_up[:, cols(n)], preferred_element_type=f32)
        sigma = jax.nn.sigmoid(gate)
        activated = gate * sigma
        act[:, cols(n)] = activated
        slope[:, cols(n)] = up * sigma * (1.0 + gate * (1.0 - sigma))
        hidden[:, cols(n)] = (activated * up).astype(bf16)
        return 0

    lax.fori_loop(0, ff // WIDE, forward, 0)
    across_ff = (((1,), (1,)), ((), ()))

    def project(n, _):
        rows_tmp[:, cols(n)] = lax.dot_general(
            hidden[...], w_down[cols(n), :], across_ff, preferred_element_type=f32
        ).astype(bf16)
        return 0

    lax.fori_loop(0, width // WIDE, project, 0)
    to_tiles(rows_tmp, sent.at[Y])
    exchange(Y)

    arrived(DY)
    to_rows(got.at[DY], rows_dy)

    def backward(n, _):
        d_hidden = jnp.dot(rows_dy[...], w_down[:, cols(n)], preferred_element_type=f32)
        d_gate[:, cols(n)] = (d_hidden * slope[:, cols(n)]).astype(bf16)
        d_up[:, cols(n)] = (d_hidden * act[:, cols(n)]).astype(bf16)
        return 0

    lax.fori_loop(0, ff // WIDE, backward, 0)

    def project_back(n, _):
        rows_tmp[:, cols(n)] = (
            lax.dot_general(d_gate[...], w_gate[cols(n), :], across_ff, preferred_element_type=f32)
            + lax.dot_general(d_up[...], w_up[cols(n), :], across_ff, preferred_element_type=f32)
        ).astype(bf16)
        return 0

    lax.fori_loop(0, width // WIDE, project_back, 0)
    to_tiles(rows_tmp, sent.at[DX])
    exchange(DX)

    def outer(n, _):
        part[cols(n), :] = lax.dot_general(
            rows_dy[:, cols(n)], hidden[...], (((0,), (0,)), ((), ())), preferred_element_type=f32
        ).astype(bf16)
        return 0

    lax.fori_loop(0, width // WIDE, outer, 0)
    pltpu.make_async_copy(part.at[owner_rows(dp)], parts.at[owner_rows(dp)], own_sem.at[4]).start()
    for k in range(1, n_dp):
        peer = (dp + k) % n_dp
        pltpu.make_async_remote_copy(
            part.at[owner_rows(peer)],
            parts.at[owner_rows(dp)],
            p_send,
            p_recv,
            device_id=(peer, e),
            device_id_type=MESH,
        ).start()

    token_col = lax.broadcasted_iota(jnp.int32, (tokens_ref.shape[0], rows), 1)
    home0 = jnp.where(token_col == row_of_col_ref[:, 0:1], 1.0, 0.0).astype(bf16)
    home1 = jnp.where(token_col == row_of_col_ref[:, 1:2], 1.0, 0.0).astype(bf16)

    arrived(Y)
    to_rows(got.at[Y], rows_tmp)

    def combine(n, _):
        first = jnp.dot(home0, rows_tmp[:, cols(n)], preferred_element_type=f32)
        second = jnp.dot(home1, rows_tmp[:, cols(n)], preferred_element_type=f32)
        moe_ref[:, cols(n)] = (
            gate_of_col_ref[:, 0:1] * first + gate_of_col_ref[:, 1:2] * second
        ).astype(bf16)
        return 0

    lax.fori_loop(0, width // WIDE, combine, 0)

    others = pl.ds(0, (n_dp - 1) * shard)
    pltpu.make_async_remote_copy(
        part.at[others], parts.at[others], p_send, p_recv, device_id=(partner, e), device_id_type=MESH
    ).wait_recv()
    pltpu.make_async_copy(part.at[owner_rows(dp)], parts.at[owner_rows(dp)], own_sem.at[4]).wait()

    def total(n, _):
        acc = None
        for p in range(n_dp):
            r = pl.ds(pl.multiple_of(p * shard + n * 32, 32), 32)
            term = parts[r, :].astype(f32)
            acc = term if acc is None else acc + term
        dgrad_ref[pl.ds(pl.multiple_of(n * 32, 32), 32), :] = acc.astype(bf16)
        return 0

    lax.fori_loop(0, shard // 32, total, 0)

    arrived(DX)
    to_rows(got.at[DX], rows_tmp)
    home = home0 + home1

    def collect(n, _):
        tgrad_ref[:, cols(n)] = jnp.dot(
            home, rows_tmp[:, cols(n)], preferred_element_type=f32
        ).astype(bf16)
        return 0

    lax.fori_loop(0, width // WIDE, collect, 0)

    for ph in range(4):
        drained(ph)
    for kind, src, full in stages:
        own3, on4 = pl.ds(0, 3 * shard), pl.ds(0, 4 * shard)
        pltpu.make_async_remote_copy(
            full.at[own3], full.at[own3], w_send.at[kind], w_recv.at[kind, dp],
            device_id=(partner, e), device_id_type=MESH,
        ).wait_send()
        pltpu.make_async_remote_copy(
            full.at[on4], full.at[on4], w_pass.at[kind], w_recv.at[kind, dp],
            device_id=(partner, e), device_id_type=MESH,
        ).wait_send()
    pltpu.make_async_remote_copy(
        part.at[others], parts.at[others], p_send, p_recv, device_id=(partner, e), device_id_type=MESH
    ).wait_send()


def per_device(tokens, out_grad, route_gates, route_slot, gate_weight, up_weight, down_weight):
    tok_dev, width = tokens.shape
    top = route_slot.shape[1]
    n_exp = lax.axis_size("expert")
    n_dp = lax.axis_size("dp")
    cap = max(2, (5 * tok_dev * top + 4 * n_exp - 1) // (4 * n_exp))
    rows = n_exp * cap
    ff = gate_weight.shape[2]
    shard = width // n_dp
    slots = route_slot.reshape(-1)
    order = jnp.arange(slots.shape[0], dtype=jnp.int32)
    earlier = (slots[:, None] == slots[None, :]) & (order[None, :] < order[:, None])
    row_of = slots * cap + jnp.sum(earlier.astype(jnp.int32), axis=1)
    row_of = row_of.reshape(tok_dev, top)

    bf16, f32 = jnp.bfloat16, jnp.float32
    vmem = pl.BlockSpec(memory_space=pltpu.VMEM)
    away = pl.BlockSpec(memory_space=pl.ANY)
    dma = pltpu.SemaphoreType.DMA
    flat = rows * SUB
    moe, tgrad, dgrad = pl.pallas_call(
        functools.partial(layer, cap),
        out_shape=(
            jax.ShapeDtypeStruct((tok_dev, width), bf16),
            jax.ShapeDtypeStruct((tok_dev, width), bf16),
            jax.ShapeDtypeStruct((shard, ff), bf16),
        ),
        in_specs=[vmem] * 6 + [away] * 3,
        out_specs=(vmem, vmem, vmem),
        scratch_shapes=[
            pltpu.VMEM((WIDE, WIDE), bf16),
            pltpu.VMEM((width, ff), bf16),
            pltpu.VMEM((width, ff), bf16),
            pltpu.VMEM((width, ff), bf16),
            pltpu.VMEM((4, flat, LANES), bf16),
            pltpu.VMEM((4, flat, LANES), bf16),
            pltpu.VMEM((rows, width), bf16),
            pltpu.VMEM((rows, width), bf16),
            pltpu.VMEM((rows, width), bf16),
            pltpu.VMEM((rows, ff), f32),
            pltpu.VMEM((rows, ff), f32),
            pltpu.VMEM((rows, ff), bf16),
            pltpu.VMEM((rows, ff), bf16),
            pltpu.VMEM((rows, ff), bf16),
            pltpu.VMEM((width, ff), bf16),
            pltpu.VMEM((width, ff), bf16),
            dma((4,)),
            dma((4,)),
            dma((5,)),
            dma((3,)),
            dma((3,)),
            dma((3,)),
            dma((3, n_dp)),
            dma,
            dma,
        ],
        name="expert_layer",
        compiler_params=pltpu.CompilerParams(
            collective_id=0, has_side_effects=True, vmem_limit_bytes=60 * 1024 * 1024
        ),
    )(
        row_of.T,
        route_gates.T,
        row_of,
        route_gates,
        tokens,
        out_grad,
        gate_weight[0],
        up_weight[0],
        down_weight[0],
    )
    return moe, tgrad, dgrad[None]


def solution(mesh):
    rows = P(("dp", "expert"), None)
    weights = P("expert", "dp", None)
    return jax.shard_map(
        per_device,
        mesh=mesh,
        in_specs=(rows, rows, rows, rows, weights, weights, weights),
        out_specs=(rows, rows, weights),
        check_vma=False,
    )
```

```python
import functools

import jax
import jax.numpy as jnp
from jax import lax
from jax.experimental import pallas as pl
from jax.experimental.pallas import tpu as pltpu
from jax.sharding import PartitionSpec as P

LANES = 128
SUB = 16
NX, NY, NZ = 4, 4, 16
WIDE = 256
MESH = pl.DeviceIdType.MESH
X, DY, Y, DX = range(4)


def layer(
    cap,
    slots_ref,
    gates_ref,
    tokens_ref,
    grads_ref,
    gate_in,
    up_in,
    down_in,
    moe_ref,
    tgrad_ref,
    dgrad_ref,
    perm,
    w_gate,
    w_up,
    w_down,
    sent,
    got,
    rows_x,
    rows_dy,
    rows_tmp,
    slope,
    act,
    hidden,
    d_gate,
    d_up,
    part,
    parts,
    send_sem,
    recv_sem,
    own_sem,
    w_own,
    w_send,
    w_pass,
    w_recv,
    p_send,
    p_recv,
):
    f32, bf16 = jnp.float32, jnp.bfloat16
    dp, e = lax.axis_index("dp"), lax.axis_index("expert")
    y, z = e // NZ, e % NZ
    chip, core = dp // 2, dp % 2
    n_exp, n_dp = NY * NZ, NX * 2
    rows = n_exp * cap
    width = tokens_ref.shape[1]
    shard = width // n_dp
    ff = hidden.shape[1]
    unit = cap * SUB

    barrier = pltpu.get_barrier_semaphore()

    def greet(k, _):
        pl.semaphore_signal(
            barrier, inc=1, device_id=(dp, (e + k) % n_exp), device_id_type=MESH
        )
        return 0

    lax.fori_loop(1, n_exp, greet, 0)
    for k in range(1, n_dp):
        pl.semaphore_signal(barrier, inc=1, device_id=((dp + k) % n_dp, e), device_id_type=MESH)

    def block(p):
        return pl.ds(pl.multiple_of(p * unit, SUB), unit)

    def owner_rows(p):
        return pl.ds(pl.multiple_of(p * shard, shard), shard)

    def cols(n):
        return pl.ds(pl.multiple_of(n * WIDE, WIDE), WIDE)

    at = lax.broadcasted_iota(jnp.int32, (WIDE, WIDE), 0)
    to = lax.broadcasted_iota(jnp.int32, (WIDE, WIDE), 1)
    perm[...] = jnp.where((at % SUB) * SUB + at // SUB == to, 1.0, 0.0).astype(bf16)

    def to_tiles(nat, flat):
        def step(g, _):
            halves = []
            for h in range(2):
                r = pl.ds(pl.multiple_of(g * 32 + h * SUB, SUB), SUB)
                halves.append(
                    jnp.concatenate(
                        [nat[r, j * LANES : (j + 1) * LANES] for j in range(SUB)], axis=0
                    )
                )
            moved = jnp.dot(
                perm[...], jnp.concatenate(halves, axis=1), preferred_element_type=f32
            ).astype(bf16)
            for h in range(2):
                r = pl.ds(pl.multiple_of(g * 512 + h * WIDE, WIDE), WIDE)
                flat[r, :] = moved[:, h * LANES : (h + 1) * LANES]
            return 0

        lax.fori_loop(0, rows // 32, step, 0)

    def to_rows(flat, nat):
        def step(g, _):
            halves = [
                flat[pl.ds(pl.multiple_of(g * 512 + h * WIDE, WIDE), WIDE), :] for h in range(2)
            ]
            moved = jnp.dot(
                perm[...], jnp.concatenate(halves, axis=1), preferred_element_type=f32
            ).astype(bf16)
            for h in range(2):
                r = pl.ds(pl.multiple_of(g * 32 + h * SUB, SUB), SUB)
                for j in range(SUB):
                    nat[r, j * LANES : (j + 1) * LANES] = moved[
                        j * SUB : (j + 1) * SUB, h * LANES : (h + 1) * LANES
                    ]
            return 0

        lax.fori_loop(0, rows // 32, step, 0)

    def send(ph, p):
        pltpu.make_async_remote_copy(
            sent.at[ph, block(p)],
            got.at[ph, block(e)],
            send_sem.at[ph],
            recv_sem.at[ph],
            device_id=(dp, p),
            device_id_type=MESH,
        ).start()

    def exchange(ph):
        pltpu.make_async_copy(
            sent.at[ph, block(e)], got.at[ph, block(e)], own_sem.at[ph]
        ).start()
        for a in range(1, NY):
            send(ph, (y + a) % NY * NZ + z)

        def step(i, _):
            for a in range(NY):
                send(ph, (y + a) % NY * NZ + (z + i) % NZ)
            return 0

        lax.fori_loop(1, NZ, step, 0)

    next_e = y * NZ + (z + 1) % NZ

    def arrived(ph):
        most = pl.ds(0, (n_exp - 1) * unit)
        pltpu.make_async_remote_copy(
            sent.at[ph, most],
            got.at[ph, most],
            send_sem.at[ph],
            recv_sem.at[ph],
            device_id=(dp, next_e),
            device_id_type=MESH,
        ).wait_recv()
        pltpu.make_async_copy(
            sent.at[ph, block(e)], got.at[ph, block(e)], own_sem.at[ph]
        ).wait()

    def drained(ph):
        most = pl.ds(0, (n_exp - 1) * unit)
        pltpu.make_async_remote_copy(
            sent.at[ph, most],
            got.at[ph, most],
            send_sem.at[ph],
            recv_sem.at[ph],
            device_id=(dp, next_e),
            device_id_type=MESH,
        ).wait_send()

    tok = tokens_ref.shape[0]
    down_to = lax.broadcasted_iota(jnp.int32, (tok, tok), 0)
    across_to = lax.broadcasted_iota(jnp.int32, (tok, tok), 1)

    def column(line):
        return jnp.sum(
            jnp.where(down_to == across_to, line, jnp.zeros_like(line)), axis=1, keepdims=True
        )

    lines = [slots_ref[k : k + 1, :] for k in range(2)]
    columns = [column(line) for line in lines]
    row_of = []
    for line in lines:
        same = (columns[0] == line) | (columns[1] == line)
        rank = jnp.sum(
            jnp.where(same & (down_to < across_to), 1, 0).astype(jnp.int32), axis=0, keepdims=True
        )
        row_of.append(line * cap + rank)

    slot_row = lax.broadcasted_iota(jnp.int32, (rows, tok), 0)
    hit0 = slot_row == row_of[0]
    hit1 = slot_row == row_of[1]
    pick = jnp.where(hit0 | hit1, 1.0, 0.0).astype(bf16)

    def gather_x(n, _):
        rows_tmp[:, cols(n)] = jnp.dot(
            pick, tokens_ref[:, cols(n)], preferred_element_type=f32
        ).astype(bf16)
        return 0

    lax.fori_loop(0, width // WIDE, gather_x, 0)
    to_tiles(rows_tmp, sent.at[X])

    pl.semaphore_wait(barrier, n_exp - 1 + n_dp - 1)

    turn = 1 - 2 * core
    partner = chip * 2 + 1 - core
    ahead = (chip + NX + turn) % NX * 2 + core
    behind = (chip + NX - turn) % NX * 2 + core
    across = (chip + 2) % NX * 2 + core
    stages = ((0, gate_in, w_gate), (1, up_in, w_up), (2, down_in, w_down))
    for kind, src, full in stages:
        pltpu.make_async_copy(src, full.at[owner_rows(dp)], w_own.at[kind]).start()
        for peer in (ahead, behind, partner):
            pltpu.make_async_remote_copy(
                src,
                full.at[owner_rows(dp)],
                w_send.at[kind],
                w_recv.at[kind, dp],
                device_id=(peer, e),
                device_id_type=MESH,
            ).start()

    exchange(X)

    def weight_in(kind, full, owner):
        pltpu.make_async_remote_copy(
            full.at[owner_rows(owner)],
            full.at[owner_rows(owner)],
            w_pass.at[kind],
            w_recv.at[kind, owner],
            device_id=(partner, e),
            device_id_type=MESH,
        ).wait_recv()

    def weight_on(kind, full, owner, peer):
        pltpu.make_async_remote_copy(
            full.at[owner_rows(owner)],
            full.at[owner_rows(owner)],
            w_pass.at[kind],
            w_recv.at[kind, owner],
            device_id=(peer, e),
            device_id_type=MESH,
        ).start()

    share = jnp.sum(
        jnp.where(hit0, gates_ref[0:1, :], 0.0) + jnp.where(hit1, gates_ref[1:2, :], 0.0),
        axis=1,
        keepdims=True,
    )

    def gather_dy(n, _):
        taken = jnp.dot(pick, grads_ref[:, cols(n)], preferred_element_type=f32)
        rows_tmp[:, cols(n)] = (share * taken).astype(bf16)
        return 0

    lax.fori_loop(0, width // WIDE, gather_dy, 0)
    to_tiles(rows_tmp, sent.at[DY])
    exchange(DY)

    for kind, _, full in stages:
        weight_in(kind, full, behind)
        weight_on(kind, full, behind, ahead)
        weight_on(kind, full, behind, partner)
        weight_in(kind, full, ahead)
        weight_on(kind, full, ahead, partner)

    for kind, _, full in stages:
        weight_in(kind, full, across)
        weight_on(kind, full, across, partner)
    for kind, src, full in stages:
        pltpu.make_async_copy(src, full.at[owner_rows(dp)], w_own.at[kind]).wait()
        for k in range(NX):
            weight_in(kind, full, (chip + k) % NX * 2 + 1 - core)

    arrived(X)
    to_rows(got.at[X], rows_x)

    def forward(n, _):
        gate = jnp.dot(rows_x[...], w_gate[:, cols(n)], preferred_element_type=f32)
        up = jnp.dot(rows_x[...], w_up[:, cols(n)], preferred_element_type=f32)
        sigma = jax.nn.sigmoid(gate)
        activated = gate * sigma
        act[:, cols(n)] = activated
        slope[:, cols(n)] = up * sigma * (1.0 + gate * (1.0 - sigma))
        hidden[:, cols(n)] = (activated * up).astype(bf16)
        return 0

    lax.fori_loop(0, ff // WIDE, forward, 0)
    across_ff = (((1,), (1,)), ((), ()))

    def project(n, _):
        rows_tmp[:, cols(n)] = lax.dot_general(
            hidden[...], w_down[cols(n), :], across_ff, preferred_element_type=f32
        ).astype(bf16)
        return 0

    lax.fori_loop(0, width // WIDE, project, 0)
    to_tiles(rows_tmp, sent.at[Y])
    exchange(Y)

    arrived(DY)
    to_rows(got.at[DY], rows_dy)

    def backward(n, _):
        d_hidden = jnp.dot(rows_dy[...], w_down[:, cols(n)], preferred_element_type=f32)
        d_gate[:, cols(n)] = (d_hidden * slope[:, cols(n)]).astype(bf16)
        d_up[:, cols(n)] = (d_hidden * act[:, cols(n)]).astype(bf16)
        return 0

    lax.fori_loop(0, ff // WIDE, backward, 0)

    def project_back(n, _):
        rows_tmp[:, cols(n)] = (
            lax.dot_general(d_gate[...], w_gate[cols(n), :], across_ff, preferred_element_type=f32)
            + lax.dot_general(d_up[...], w_up[cols(n), :], across_ff, preferred_element_type=f32)
        ).astype(bf16)
        return 0

    lax.fori_loop(0, width // WIDE, project_back, 0)
    to_tiles(rows_tmp, sent.at[DX])
    exchange(DX)

    def outer(n, _):
        part[cols(n), :] = lax.dot_general(
            rows_dy[:, cols(n)], hidden[...], (((0,), (0,)), ((), ())), preferred_element_type=f32
        ).astype(bf16)
        return 0

    lax.fori_loop(0, width // WIDE, outer, 0)
    pltpu.make_async_copy(part.at[owner_rows(dp)], parts.at[owner_rows(dp)], own_sem.at[4]).start()
    for k in range(1, n_dp):
        peer = (dp + k) % n_dp
        pltpu.make_async_remote_copy(
            part.at[owner_rows(peer)],
            parts.at[owner_rows(dp)],
            p_send,
            p_recv,
            device_id=(peer, e),
            device_id_type=MESH,
        ).start()

    token_col = lax.broadcasted_iota(jnp.int32, (tok, rows), 1)
    home0 = jnp.where(token_col == column(row_of[0]), 1.0, 0.0).astype(bf16)
    home1 = jnp.where(token_col == column(row_of[1]), 1.0, 0.0).astype(bf16)

    gate0, gate1 = column(gates_ref[0:1, :]), column(gates_ref[1:2, :])

    arrived(Y)
    to_rows(got.at[Y], rows_tmp)

    def combine(n, _):
        first = jnp.dot(home0, rows_tmp[:, cols(n)], preferred_element_type=f32)
        second = jnp.dot(home1, rows_tmp[:, cols(n)], preferred_element_type=f32)
        moe_ref[:, cols(n)] = (
            gate0 * first + gate1 * second
        ).astype(bf16)
        return 0

    lax.fori_loop(0, width // WIDE, combine, 0)

    others = pl.ds(0, (n_dp - 1) * shard)
    pltpu.make_async_remote_copy(
        part.at[others], parts.at[others], p_send, p_recv, device_id=(partner, e), device_id_type=MESH
    ).wait_recv()
    pltpu.make_async_copy(part.at[owner_rows(dp)], parts.at[owner_rows(dp)], own_sem.at[4]).wait()

    def total(n, _):
        acc = None
        for p in range(n_dp):
            r = pl.ds(pl.multiple_of(p * shard + n * 32, 32), 32)
            term = parts[r, :].astype(f32)
            acc = term if acc is None else acc + term
        dgrad_ref[pl.ds(pl.multiple_of(n * 32, 32), 32), :] = acc.astype(bf16)
        return 0

    lax.fori_loop(0, shard // 32, total, 0)

    arrived(DX)
    to_rows(got.at[DX], rows_tmp)
    home = home0 + home1

    def collect(n, _):
        tgrad_ref[:, cols(n)] = jnp.dot(
            home, rows_tmp[:, cols(n)], preferred_element_type=f32
        ).astype(bf16)
        return 0

    lax.fori_loop(0, width // WIDE, collect, 0)

    for ph in range(4):
        drained(ph)
    for kind, src, full in stages:
        own3, on4 = pl.ds(0, 3 * shard), pl.ds(0, 4 * shard)
        pltpu.make_async_remote_copy(
            full.at[own3], full.at[own3], w_send.at[kind], w_recv.at[kind, dp],
            device_id=(partner, e), device_id_type=MESH,
        ).wait_send()
        pltpu.make_async_remote_copy(
            full.at[on4], full.at[on4], w_pass.at[kind], w_recv.at[kind, dp],
            device_id=(partner, e), device_id_type=MESH,
        ).wait_send()
    pltpu.make_async_remote_copy(
        part.at[others], parts.at[others], p_send, p_recv, device_id=(partner, e), device_id_type=MESH
    ).wait_send()


def per_device(tokens, out_grad, route_gates, route_slot, gate_weight, up_weight, down_weight):
    tok_dev, width = tokens.shape
    top = route_slot.shape[1]
    n_exp = lax.axis_size("expert")
    n_dp = lax.axis_size("dp")
    cap = max(2, (5 * tok_dev * top + 4 * n_exp - 1) // (4 * n_exp))
    rows = n_exp * cap
    ff = gate_weight.shape[2]
    shard = width // n_dp
    bf16, f32 = jnp.bfloat16, jnp.float32
    vmem = pl.BlockSpec(memory_space=pltpu.VMEM)
    away = pl.BlockSpec(memory_space=pl.ANY)
    dma = pltpu.SemaphoreType.DMA
    flat = rows * SUB
    moe, tgrad, dgrad = pl.pallas_call(
        functools.partial(layer, cap),
        out_shape=(
            pltpu.VMEM((tok_dev, width), bf16),
            pltpu.VMEM((tok_dev, width), bf16),
            pltpu.VMEM((shard, ff), bf16),
        ),
        in_specs=[vmem] * 4 + [away] * 3,
        out_specs=(vmem, vmem, vmem),
        scratch_shapes=[
            pltpu.VMEM((WIDE, WIDE), bf16),
            pltpu.VMEM((width, ff), bf16),
            pltpu.VMEM((width, ff), bf16),
            pltpu.VMEM((width, ff), bf16),
            pltpu.VMEM((4, flat, LANES), bf16),
            pltpu.VMEM((4, flat, LANES), bf16),
            pltpu.VMEM((rows, width), bf16),
            pltpu.VMEM((rows, width), bf16),
            pltpu.VMEM((rows, width), bf16),
            pltpu.VMEM((rows, ff), f32),
            pltpu.VMEM((rows, ff), f32),
            pltpu.VMEM((rows, ff), bf16),
            pltpu.VMEM((rows, ff), bf16),
            pltpu.VMEM((rows, ff), bf16),
            pltpu.VMEM((width, ff), bf16),
            pltpu.VMEM((width, ff), bf16),
            dma((4,)),
            dma((4,)),
            dma((5,)),
            dma((3,)),
            dma((3,)),
            dma((3,)),
            dma((3, n_dp)),
            dma,
            dma,
        ],
        name="expert_layer",
        compiler_params=pltpu.CompilerParams(
            collective_id=0, has_side_effects=True, vmem_limit_bytes=60 * 1024 * 1024
        ),
    )(
        route_slot.T,
        route_gates.T,
        tokens,
        out_grad,
        gate_weight[0],
        up_weight[0],
        down_weight[0],
    )
    return moe, tgrad, dgrad[None]


def solution(mesh):
    rows = P(("dp", "expert"), None)
    weights = P("expert", "dp", None)
    return jax.shard_map(
        per_device,
        mesh=mesh,
        in_specs=(rows, rows, rows, rows, weights, weights, weights),
        out_specs=(rows, rows, weights),
        check_vma=False,
    )
```

```python
import functools

import jax
import jax.numpy as jnp
from jax import lax
from jax.experimental import pallas as pl
from jax.experimental.pallas import tpu as pltpu
from jax.sharding import PartitionSpec as P

LANES = 128
SUB = 16
NX, NY, NZ = 4, 4, 16
WIDE = 256
MESH = pl.DeviceIdType.MESH
X, DY, Y, DX = range(4)


def layer(
    cap,
    slots_ref,
    gates_ref,
    tokens_ref,
    grads_ref,
    gate_in,
    up_in,
    down_in,
    moe_ref,
    tgrad_ref,
    dgrad_ref,
    perm,
    w_gate,
    w_up,
    w_down,
    sent,
    got,
    rows_x,
    rows_dy,
    rows_tmp,
    slope,
    act,
    hidden,
    d_gate,
    d_up,
    part,
    parts,
    send_sem,
    recv_sem,
    own_sem,
    w_own,
    w_send,
    w_pass,
    w_recv,
    p_send,
    p_recv,
    near,
):
    f32, bf16 = jnp.float32, jnp.bfloat16
    dp, e = lax.axis_index("dp"), lax.axis_index("expert")
    y, z = e // NZ, e % NZ
    chip, core = dp // 2, dp % 2
    n_exp, n_dp = NY * NZ, NX * 2
    rows = n_exp * cap
    width = tokens_ref.shape[1]
    shard = width // n_dp
    ff = hidden.shape[1]
    unit = cap * SUB

    barrier = pltpu.get_barrier_semaphore()

    above = y * NZ + (z + 1) % NZ
    below = y * NZ + (z + NZ - 1) % NZ
    for a in range(1, NY):
        pl.semaphore_signal(
            barrier, inc=1, device_id=(dp, (y + a) % NY * NZ + z), device_id_type=MESH
        )
    for p in (above, below):
        pl.semaphore_signal(barrier, inc=1, device_id=(dp, p), device_id_type=MESH)
    for k in range(1, n_dp):
        pl.semaphore_signal(barrier, inc=1, device_id=((dp + k) % n_dp, e), device_id_type=MESH)

    def tell():
        pl.semaphore_signal(near.at[0], inc=1, device_id=(dp, above), device_id_type=MESH)
        pl.semaphore_signal(near.at[1], inc=1, device_id=(dp, below), device_id_type=MESH)

    def meet():
        pl.semaphore_wait(near.at[0], 1)
        pl.semaphore_wait(near.at[1], 1)

    def block(p):
        return pl.ds(pl.multiple_of(p * unit, SUB), unit)

    def owner_rows(p):
        return pl.ds(pl.multiple_of(p * shard, shard), shard)

    def cols(n):
        return pl.ds(pl.multiple_of(n * WIDE, WIDE), WIDE)

    at = lax.broadcasted_iota(jnp.int32, (WIDE, WIDE), 0)
    to = lax.broadcasted_iota(jnp.int32, (WIDE, WIDE), 1)
    perm[...] = jnp.where((at % SUB) * SUB + at // SUB == to, 1.0, 0.0).astype(bf16)

    def to_tiles(nat, flat, first=0, last=rows // 32, unroll=False):
        def step(g, _):
            halves = []
            for h in range(2):
                r = pl.ds(pl.multiple_of(g * 32 + h * SUB, SUB), SUB)
                halves.append(
                    jnp.concatenate(
                        [nat[r, j * LANES : (j + 1) * LANES] for j in range(SUB)], axis=0
                    )
                )
            moved = jnp.dot(
                perm[...], jnp.concatenate(halves, axis=1), preferred_element_type=f32
            ).astype(bf16)
            for h in range(2):
                r = pl.ds(pl.multiple_of(g * 512 + h * WIDE, WIDE), WIDE)
                flat[r, :] = moved[:, h * LANES : (h + 1) * LANES]
            return 0

        lax.fori_loop(first, last, step, 0, unroll=unroll)

    def to_rows(flat, nat, unroll=False):
        def step(g, _):
            halves = [
                flat[pl.ds(pl.multiple_of(g * 512 + h * WIDE, WIDE), WIDE), :] for h in range(2)
            ]
            moved = jnp.dot(
                perm[...], jnp.concatenate(halves, axis=1), preferred_element_type=f32
            ).astype(bf16)
            for h in range(2):
                r = pl.ds(pl.multiple_of(g * 32 + h * SUB, SUB), SUB)
                for j in range(SUB):
                    nat[r, j * LANES : (j + 1) * LANES] = moved[
                        j * SUB : (j + 1) * SUB, h * LANES : (h + 1) * LANES
                    ]
            return 0

        lax.fori_loop(0, rows // 32, step, 0, unroll=unroll)

    def send(ph, p):
        pltpu.make_async_remote_copy(
            sent.at[ph, block(p)],
            got.at[ph, block(e)],
            send_sem.at[ph],
            recv_sem.at[ph],
            device_id=(dp, p),
            device_id_type=MESH,
        ).start()

    def exchange(ph):
        pltpu.make_async_copy(
            sent.at[ph, block(e)], got.at[ph, block(e)], own_sem.at[ph]
        ).start()
        for a in range(1, NY):
            send(ph, (y + a) % NY * NZ + z)

        def step(i, _):
            for a in range(NY):
                send(ph, (y + a) % NY * NZ + (z + i) % NZ)
            return 0

        lax.fori_loop(1, NZ, step, 0)

    next_e = y * NZ + (z + 1) % NZ

    def arrived(ph):
        most = pl.ds(0, (n_exp - 1) * unit)
        pltpu.make_async_remote_copy(
            sent.at[ph, most],
            got.at[ph, most],
            send_sem.at[ph],
            recv_sem.at[ph],
            device_id=(dp, next_e),
            device_id_type=MESH,
        ).wait_recv()
        pltpu.make_async_copy(
            sent.at[ph, block(e)], got.at[ph, block(e)], own_sem.at[ph]
        ).wait()

    def drained(ph):
        most = pl.ds(0, (n_exp - 1) * unit)
        pltpu.make_async_remote_copy(
            sent.at[ph, most],
            got.at[ph, most],
            send_sem.at[ph],
            recv_sem.at[ph],
            device_id=(dp, next_e),
            device_id_type=MESH,
        ).wait_send()

    tok = tokens_ref.shape[0]
    down_to = lax.broadcasted_iota(jnp.int32, (tok, tok), 0)
    across_to = lax.broadcasted_iota(jnp.int32, (tok, tok), 1)

    def column(line):
        return jnp.sum(
            jnp.where(down_to == across_to, line, jnp.zeros_like(line)), axis=1, keepdims=True
        )

    lines = [slots_ref[k : k + 1, :] for k in range(2)]
    columns = [column(line) for line in lines]
    row_of = []
    for line in lines:
        same = (columns[0] == line) | (columns[1] == line)
        rank = jnp.sum(
            jnp.where(same & (down_to < across_to), 1, 0).astype(jnp.int32), axis=0, keepdims=True
        )
        row_of.append(line * cap + rank)

    slot_row = lax.broadcasted_iota(jnp.int32, (rows, tok), 0)
    hit0 = slot_row == row_of[0]
    hit1 = slot_row == row_of[1]
    pick = jnp.where(hit0 | hit1, 1.0, 0.0).astype(bf16)

    def gather_x(n, _):
        rows_tmp[:, cols(n)] = jnp.dot(
            pick, tokens_ref[:, cols(n)], preferred_element_type=f32
        ).astype(bf16)
        return 0

    pl.semaphore_wait(barrier, NY - 1 + 2 + n_dp - 1)
    tell()
    lax.fori_loop(0, width // WIDE, gather_x, 0, unroll=True)
    meet()
    tell()
    to_tiles(rows_tmp, sent.at[X], 0, rows // 64, True)
    meet()
    tell()
    to_tiles(rows_tmp, sent.at[X], rows // 64, rows // 32, True)
    meet()
    tell()

    turn = 1 - 2 * core
    partner = chip * 2 + 1 - core
    ahead = (chip + NX + turn) % NX * 2 + core
    behind = (chip + NX - turn) % NX * 2 + core
    across = (chip + 2) % NX * 2 + core
    stages = ((0, gate_in, w_gate), (1, up_in, w_up), (2, down_in, w_down))
    for kind, src, full in stages:
        pltpu.make_async_copy(src, full.at[owner_rows(dp)], w_own.at[kind]).start()
        for peer in (ahead, behind, partner):
            pltpu.make_async_remote_copy(
                src,
                full.at[owner_rows(dp)],
                w_send.at[kind],
                w_recv.at[kind, dp],
                device_id=(peer, e),
                device_id_type=MESH,
            ).start()

    pltpu.make_async_copy(sent.at[X, block(e)], got.at[X, block(e)], own_sem.at[X]).start()
    for a in range(1, NY):
        send(X, (y + a) % NY * NZ + z)
    for k in range(1, NZ // 2 + 1):
        if k > 3:
            meet()
            if k < NZ // 2:
                tell()
        for a in range(NY):
            send(X, (y + a) % NY * NZ + (z + k) % NZ)
            if k < NZ // 2:
                send(X, (y + a) % NY * NZ + (z + NZ - k) % NZ)

    def weight_in(kind, full, owner):
        pltpu.make_async_remote_copy(
            full.at[owner_rows(owner)],
            full.at[owner_rows(owner)],
            w_pass.at[kind],
            w_recv.at[kind, owner],
            device_id=(partner, e),
            device_id_type=MESH,
        ).wait_recv()

    def weight_on(kind, full, owner, peer):
        pltpu.make_async_remote_copy(
            full.at[owner_rows(owner)],
            full.at[owner_rows(owner)],
            w_pass.at[kind],
            w_recv.at[kind, owner],
            device_id=(peer, e),
            device_id_type=MESH,
        ).start()

    share = jnp.sum(
        jnp.where(hit0, gates_ref[0:1, :], 0.0) + jnp.where(hit1, gates_ref[1:2, :], 0.0),
        axis=1,
        keepdims=True,
    )

    def gather_dy(n, _):
        taken = jnp.dot(pick, grads_ref[:, cols(n)], preferred_element_type=f32)
        rows_tmp[:, cols(n)] = (share * taken).astype(bf16)
        return 0

    lax.fori_loop(0, width // WIDE, gather_dy, 0)
    to_tiles(rows_tmp, sent.at[DY])
    exchange(DY)

    for kind, _, full in stages:
        weight_in(kind, full, behind)
        weight_on(kind, full, behind, ahead)
        weight_on(kind, full, behind, partner)
        weight_in(kind, full, ahead)
        weight_on(kind, full, ahead, partner)

    for kind, _, full in stages:
        weight_in(kind, full, across)
        weight_on(kind, full, across, partner)
    for kind, src, full in stages:
        pltpu.make_async_copy(src, full.at[owner_rows(dp)], w_own.at[kind]).wait()
        for k in range(NX):
            weight_in(kind, full, (chip + k) % NX * 2 + 1 - core)

    arrived(X)
    to_rows(got.at[X], rows_x)

    def forward(n, _):
        gate = jnp.dot(rows_x[...], w_gate[:, cols(n)], preferred_element_type=f32)
        up = jnp.dot(rows_x[...], w_up[:, cols(n)], preferred_element_type=f32)
        sigma = jax.nn.sigmoid(gate)
        activated = gate * sigma
        act[:, cols(n)] = activated
        slope[:, cols(n)] = up * sigma * (1.0 + gate * (1.0 - sigma))
        hidden[:, cols(n)] = (activated * up).astype(bf16)
        return 0

    lax.fori_loop(0, ff // WIDE, forward, 0)
    across_ff = (((1,), (1,)), ((), ()))

    def project(n, _):
        rows_tmp[:, cols(n)] = lax.dot_general(
            hidden[...], w_down[cols(n), :], across_ff, preferred_element_type=f32
        ).astype(bf16)
        return 0

    lax.fori_loop(0, width // WIDE, project, 0)
    to_tiles(rows_tmp, sent.at[Y])
    exchange(Y)

    arrived(DY)
    to_rows(got.at[DY], rows_dy)

    def backward(n, _):
        d_hidden = jnp.dot(rows_dy[...], w_down[:, cols(n)], preferred_element_type=f32)
        d_gate[:, cols(n)] = (d_hidden * slope[:, cols(n)]).astype(bf16)
        d_up[:, cols(n)] = (d_hidden * act[:, cols(n)]).astype(bf16)
        return 0

    lax.fori_loop(0, ff // WIDE, backward, 0)

    def project_back(n, _):
        rows_tmp[:, cols(n)] = (
            lax.dot_general(d_gate[...], w_gate[cols(n), :], across_ff, preferred_element_type=f32)
            + lax.dot_general(d_up[...], w_up[cols(n), :], across_ff, preferred_element_type=f32)
        ).astype(bf16)
        return 0

    lax.fori_loop(0, width // WIDE, project_back, 0)
    to_tiles(rows_tmp, sent.at[DX])
    exchange(DX)

    def outer(n, _):
        part[cols(n), :] = lax.dot_general(
            rows_dy[:, cols(n)], hidden[...], (((0,), (0,)), ((), ())), preferred_element_type=f32
        ).astype(bf16)
        return 0

    lax.fori_loop(0, width // WIDE, outer, 0)
    pltpu.make_async_copy(part.at[owner_rows(dp)], parts.at[owner_rows(dp)], own_sem.at[4]).start()
    for k in range(1, n_dp):
        peer = (dp + k) % n_dp
        pltpu.make_async_remote_copy(
            part.at[owner_rows(peer)],
            parts.at[owner_rows(dp)],
            p_send,
            p_recv,
            device_id=(peer, e),
            device_id_type=MESH,
        ).start()

    token_col = lax.broadcasted_iota(jnp.int32, (tok, rows), 1)
    home0 = jnp.where(token_col == column(row_of[0]), 1.0, 0.0).astype(bf16)
    home1 = jnp.where(token_col == column(row_of[1]), 1.0, 0.0).astype(bf16)

    gate0, gate1 = column(gates_ref[0:1, :]), column(gates_ref[1:2, :])

    arrived(Y)
    to_rows(got.at[Y], rows_tmp)

    def combine(n, _):
        first = jnp.dot(home0, rows_tmp[:, cols(n)], preferred_element_type=f32)
        second = jnp.dot(home1, rows_tmp[:, cols(n)], preferred_element_type=f32)
        moe_ref[:, cols(n)] = (
            gate0 * first + gate1 * second
        ).astype(bf16)
        return 0

    lax.fori_loop(0, width // WIDE, combine, 0)

    others = pl.ds(0, (n_dp - 1) * shard)
    pltpu.make_async_remote_copy(
        part.at[others], parts.at[others], p_send, p_recv, device_id=(partner, e), device_id_type=MESH
    ).wait_recv()
    pltpu.make_async_copy(part.at[owner_rows(dp)], parts.at[owner_rows(dp)], own_sem.at[4]).wait()

    def total(n, _):
        acc = None
        for p in range(n_dp):
            r = pl.ds(pl.multiple_of(p * shard + n * 32, 32), 32)
            term = parts[r, :].astype(f32)
            acc = term if acc is None else acc + term
        dgrad_ref[pl.ds(pl.multiple_of(n * 32, 32), 32), :] = acc.astype(bf16)
        return 0

    lax.fori_loop(0, shard // 32, total, 0)

    arrived(DX)
    to_rows(got.at[DX], rows_tmp, True)
    home = home0 + home1

    def collect(n, _):
        tgrad_ref[:, cols(n)] = jnp.dot(
            home, rows_tmp[:, cols(n)], preferred_element_type=f32
        ).astype(bf16)
        return 0

    lax.fori_loop(0, width // WIDE, collect, 0, unroll=True)

    for ph in range(4):
        drained(ph)
    for kind, src, full in stages:
        own3, on4 = pl.ds(0, 3 * shard), pl.ds(0, 4 * shard)
        pltpu.make_async_remote_copy(
            full.at[own3], full.at[own3], w_send.at[kind], w_recv.at[kind, dp],
            device_id=(partner, e), device_id_type=MESH,
        ).wait_send()
        pltpu.make_async_remote_copy(
            full.at[on4], full.at[on4], w_pass.at[kind], w_recv.at[kind, dp],
            device_id=(partner, e), device_id_type=MESH,
        ).wait_send()
    pltpu.make_async_remote_copy(
        part.at[others], parts.at[others], p_send, p_recv, device_id=(partner, e), device_id_type=MESH
    ).wait_send()


def put(*refs):
    n = len(refs) // 2
    copies = [pltpu.make_async_copy(refs[i], refs[n + i], refs[2 * n].at[i]) for i in range(n)]
    for copy in copies:
        copy.start()
    for copy in copies:
        copy.wait()


def put_out(*arrays):
    n = len(arrays)
    return pl.pallas_call(
        put,
        out_shape=[jax.ShapeDtypeStruct(a.shape, a.dtype) for a in arrays],
        in_specs=[pl.BlockSpec(memory_space=pltpu.VMEM)] * n,
        out_specs=[pl.BlockSpec(memory_space=pl.ANY)] * n,
        scratch_shapes=[pltpu.SemaphoreType.DMA((n,))],
        name="put_out",
    )(*[pltpu.with_memory_space_constraint(a, pltpu.VMEM) for a in arrays])


def per_device(tokens, out_grad, route_gates, route_slot, gate_weight, up_weight, down_weight):
    tok_dev, width = tokens.shape
    top = route_slot.shape[1]
    n_exp = lax.axis_size("expert")
    n_dp = lax.axis_size("dp")
    cap = max(2, (5 * tok_dev * top + 4 * n_exp - 1) // (4 * n_exp))
    rows = n_exp * cap
    ff = gate_weight.shape[2]
    shard = width // n_dp
    bf16, f32 = jnp.bfloat16, jnp.float32
    vmem = pl.BlockSpec(memory_space=pltpu.VMEM)
    away = pl.BlockSpec(memory_space=pl.ANY)
    dma = pltpu.SemaphoreType.DMA
    flat = rows * SUB
    moe, tgrad, dgrad = pl.pallas_call(
        functools.partial(layer, cap),
        out_shape=(
            pltpu.VMEM((tok_dev, width), bf16),
            pltpu.VMEM((tok_dev, width), bf16),
            pltpu.VMEM((shard, ff), bf16),
        ),
        in_specs=[vmem] * 4 + [away] * 3,
        out_specs=(vmem, vmem, vmem),
        scratch_shapes=[
            pltpu.VMEM((WIDE, WIDE), bf16),
            pltpu.VMEM((width, ff), bf16),
            pltpu.VMEM((width, ff), bf16),
            pltpu.VMEM((width, ff), bf16),
            pltpu.VMEM((4, flat, LANES), bf16),
            pltpu.VMEM((4, flat, LANES), bf16),
            pltpu.VMEM((rows, width), bf16),
            pltpu.VMEM((rows, width), bf16),
            pltpu.VMEM((rows, width), bf16),
            pltpu.VMEM((rows, ff), f32),
            pltpu.VMEM((rows, ff), f32),
            pltpu.VMEM((rows, ff), bf16),
            pltpu.VMEM((rows, ff), bf16),
            pltpu.VMEM((rows, ff), bf16),
            pltpu.VMEM((width, ff), bf16),
            pltpu.VMEM((width, ff), bf16),
            dma((4,)),
            dma((4,)),
            dma((5,)),
            dma((3,)),
            dma((3,)),
            dma((3,)),
            dma((3, n_dp)),
            dma,
            dma,
            pltpu.SemaphoreType.REGULAR((2,)),
        ],
        name="expert_layer",
        compiler_params=pltpu.CompilerParams(
            collective_id=0, has_side_effects=True, vmem_limit_bytes=60 * 1024 * 1024
        ),
    )(
        route_slot.T,
        route_gates.T,
        tokens,
        out_grad,
        gate_weight[0],
        up_weight[0],
        down_weight[0],
    )
    moe, tgrad, dgrad = put_out(moe, tgrad, dgrad)
    return moe, tgrad, dgrad[None]


def solution(mesh):
    rows = P(("dp", "expert"), None)
    weights = P("expert", "dp", None)
    return jax.shard_map(
        per_device,
        mesh=mesh,
        in_specs=(rows, rows, rows, rows, weights, weights, weights),
        out_specs=(rows, rows, weights),
        check_vma=False,
    )
```

```python
import functools

import jax
import jax.numpy as jnp
from jax import lax
from jax.experimental import pallas as pl
from jax.experimental.pallas import tpu as pltpu
from jax.sharding import PartitionSpec as P

LANES = 128
SUB = 16
NX, NY, NZ = 4, 4, 16
WIDE = 256
MESH = pl.DeviceIdType.MESH
X, DY, Y, DX = range(4)


def layer(
    cap,
    slots_ref,
    gates_ref,
    tokens_ref,
    grads_ref,
    gate_in,
    up_in,
    down_in,
    moe_ref,
    tgrad_ref,
    dgrad_ref,
    perm,
    w_gate,
    w_up,
    w_down,
    sent,
    got,
    rows_x,
    rows_dy,
    rows_tmp,
    slope,
    act,
    hidden,
    d_gate,
    d_up,
    part,
    parts,
    send_sem,
    recv_sem,
    own_sem,
    w_own,
    w_send,
    w_pass,
    w_recv,
    p_send,
    p_recv,
    near,
):
    f32, bf16 = jnp.float32, jnp.bfloat16
    dp, e = lax.axis_index("dp"), lax.axis_index("expert")
    y, z = e // NZ, e % NZ
    chip, core = dp // 2, dp % 2
    n_exp, n_dp = NY * NZ, NX * 2
    rows = n_exp * cap
    width = tokens_ref.shape[1]
    shard = width // n_dp
    ff = hidden.shape[1]
    unit = cap * SUB

    barrier = pltpu.get_barrier_semaphore()

    above = y * NZ + (z + 1) % NZ
    below = y * NZ + (z + NZ - 1) % NZ
    for a in range(1, NY):
        pl.semaphore_signal(
            barrier, inc=1, device_id=(dp, (y + a) % NY * NZ + z), device_id_type=MESH
        )
    for p in (above, below):
        pl.semaphore_signal(barrier, inc=1, device_id=(dp, p), device_id_type=MESH)
    for k in range(1, n_dp):
        pl.semaphore_signal(barrier, inc=1, device_id=((dp + k) % n_dp, e), device_id_type=MESH)

    def tell():
        pl.semaphore_signal(near.at[0], inc=1, device_id=(dp, above), device_id_type=MESH)
        pl.semaphore_signal(near.at[1], inc=1, device_id=(dp, below), device_id_type=MESH)

    def meet():
        pl.semaphore_wait(near.at[0], 1)
        pl.semaphore_wait(near.at[1], 1)

    def block(p):
        return pl.ds(pl.multiple_of(p * unit, SUB), unit)

    def owner_rows(p):
        return pl.ds(pl.multiple_of(p * shard, shard), shard)

    def cols(n):
        return pl.ds(pl.multiple_of(n * WIDE, WIDE), WIDE)

    at = lax.broadcasted_iota(jnp.int32, (WIDE, WIDE), 0)
    to = lax.broadcasted_iota(jnp.int32, (WIDE, WIDE), 1)
    perm[...] = jnp.where((at % SUB) * SUB + at // SUB == to, 1.0, 0.0).astype(bf16)

    def to_tiles(nat, flat, first=0, last=rows // 32, unroll=False):
        def step(g, _):
            halves = []
            for h in range(2):
                r = pl.ds(pl.multiple_of(g * 32 + h * SUB, SUB), SUB)
                halves.append(
                    jnp.concatenate(
                        [nat[r, j * LANES : (j + 1) * LANES] for j in range(SUB)], axis=0
                    )
                )
            moved = jnp.dot(
                perm[...], jnp.concatenate(halves, axis=1), preferred_element_type=f32
            ).astype(bf16)
            for h in range(2):
                r = pl.ds(pl.multiple_of(g * 512 + h * WIDE, WIDE), WIDE)
                flat[r, :] = moved[:, h * LANES : (h + 1) * LANES]
            return 0

        lax.fori_loop(first, last, step, 0, unroll=unroll)

    def to_rows(flat, nat, unroll=False):
        def step(g, _):
            halves = [
                flat[pl.ds(pl.multiple_of(g * 512 + h * WIDE, WIDE), WIDE), :] for h in range(2)
            ]
            moved = jnp.dot(
                perm[...], jnp.concatenate(halves, axis=1), preferred_element_type=f32
            ).astype(bf16)
            for h in range(2):
                r = pl.ds(pl.multiple_of(g * 32 + h * SUB, SUB), SUB)
                for j in range(SUB):
                    nat[r, j * LANES : (j + 1) * LANES] = moved[
                        j * SUB : (j + 1) * SUB, h * LANES : (h + 1) * LANES
                    ]
            return 0

        lax.fori_loop(0, rows // 32, step, 0, unroll=unroll)

    def send(ph, p):
        pltpu.make_async_remote_copy(
            sent.at[ph, block(p)],
            got.at[ph, block(e)],
            send_sem.at[ph],
            recv_sem.at[ph],
            device_id=(dp, p),
            device_id_type=MESH,
        ).start()

    def exchange(ph):
        pltpu.make_async_copy(
            sent.at[ph, block(e)], got.at[ph, block(e)], own_sem.at[ph]
        ).start()
        def line(dz):
            for a in range(NY):
                send(ph, (y + a) % NY * NZ + (z + dz) % NZ)

        def step(i, _):
            line(7 - i)
            line(NZ - 2 - i)
            line(2 + i)
            line(NZ - 7 + i)
            return 0

        line(NZ // 2)
        lax.fori_loop(0, 3, step, 0)
        line(1)
        line(NZ - 1)
        for a in range(1, NY):
            send(ph, (y + a) % NY * NZ + z)

    next_e = y * NZ + (z + 1) % NZ

    def arrived(ph):
        most = pl.ds(0, (n_exp - 1) * unit)
        pltpu.make_async_remote_copy(
            sent.at[ph, most],
            got.at[ph, most],
            send_sem.at[ph],
            recv_sem.at[ph],
            device_id=(dp, next_e),
            device_id_type=MESH,
        ).wait_recv()
        pltpu.make_async_copy(
            sent.at[ph, block(e)], got.at[ph, block(e)], own_sem.at[ph]
        ).wait()

    def drained(ph):
        most = pl.ds(0, (n_exp - 1) * unit)
        pltpu.make_async_remote_copy(
            sent.at[ph, most],
            got.at[ph, most],
            send_sem.at[ph],
            recv_sem.at[ph],
            device_id=(dp, next_e),
            device_id_type=MESH,
        ).wait_send()

    tok = tokens_ref.shape[0]
    down_to = lax.broadcasted_iota(jnp.int32, (tok, tok), 0)
    across_to = lax.broadcasted_iota(jnp.int32, (tok, tok), 1)

    def column(line):
        return jnp.sum(
            jnp.where(down_to == across_to, line, jnp.zeros_like(line)), axis=1, keepdims=True
        )

    lines = [slots_ref[k : k + 1, :] for k in range(2)]
    columns = [column(line) for line in lines]
    row_of = []
    for line in lines:
        same = (columns[0] == line) | (columns[1] == line)
        rank = jnp.sum(
            jnp.where(same & (down_to < across_to), 1, 0).astype(jnp.int32), axis=0, keepdims=True
        )
        row_of.append(line * cap + rank)

    slot_row = lax.broadcasted_iota(jnp.int32, (rows, tok), 0)
    hit0 = slot_row == row_of[0]
    hit1 = slot_row == row_of[1]
    pick = jnp.where(hit0 | hit1, 1.0, 0.0).astype(bf16)

    def gather_x(n, _):
        rows_tmp[:, cols(n)] = jnp.dot(
            pick, tokens_ref[:, cols(n)], preferred_element_type=f32
        ).astype(bf16)
        return 0

    pl.semaphore_wait(barrier, NY - 1 + 2 + n_dp - 1)
    tell()
    lax.fori_loop(0, width // WIDE, gather_x, 0, unroll=True)
    meet()
    tell()
    to_tiles(rows_tmp, sent.at[X], 0, rows // 64, True)
    meet()
    tell()
    to_tiles(rows_tmp, sent.at[X], rows // 64, rows // 32, True)
    meet()
    tell()

    turn = 1 - 2 * core
    partner = chip * 2 + 1 - core
    ahead = (chip + NX + turn) % NX * 2 + core
    behind = (chip + NX - turn) % NX * 2 + core
    across = (chip + 2) % NX * 2 + core
    stages = ((0, gate_in, w_gate), (1, up_in, w_up), (2, down_in, w_down))
    for kind, src, full in stages:
        pltpu.make_async_copy(src, full.at[owner_rows(dp)], w_own.at[kind]).start()
        for peer in (ahead, behind, partner):
            pltpu.make_async_remote_copy(
                src,
                full.at[owner_rows(dp)],
                w_send.at[kind],
                w_recv.at[kind, dp],
                device_id=(peer, e),
                device_id_type=MESH,
            ).start()

    pltpu.make_async_copy(sent.at[X, block(e)], got.at[X, block(e)], own_sem.at[X]).start()
    for a in range(1, NY):
        send(X, (y + a) % NY * NZ + z)
    for k in range(1, NZ // 2 + 1):
        if k > 3:
            meet()
            if k < NZ // 2:
                tell()
        for a in range(NY):
            send(X, (y + a) % NY * NZ + (z + k) % NZ)
            if k < NZ // 2:
                send(X, (y + a) % NY * NZ + (z + NZ - k) % NZ)

    def weight_in(kind, full, owner):
        pltpu.make_async_remote_copy(
            full.at[owner_rows(owner)],
            full.at[owner_rows(owner)],
            w_pass.at[kind],
            w_recv.at[kind, owner],
            device_id=(partner, e),
            device_id_type=MESH,
        ).wait_recv()

    def weight_on(kind, full, owner, peer):
        pltpu.make_async_remote_copy(
            full.at[owner_rows(owner)],
            full.at[owner_rows(owner)],
            w_pass.at[kind],
            w_recv.at[kind, owner],
            device_id=(peer, e),
            device_id_type=MESH,
        ).start()

    share = jnp.sum(
        jnp.where(hit0, gates_ref[0:1, :], 0.0) + jnp.where(hit1, gates_ref[1:2, :], 0.0),
        axis=1,
        keepdims=True,
    )

    def gather_dy(n, _):
        taken = jnp.dot(pick, grads_ref[:, cols(n)], preferred_element_type=f32)
        rows_tmp[:, cols(n)] = (share * taken).astype(bf16)
        return 0

    lax.fori_loop(0, width // WIDE, gather_dy, 0)
    to_tiles(rows_tmp, sent.at[DY])
    exchange(DY)

    for kind, _, full in stages:
        weight_in(kind, full, behind)
        weight_on(kind, full, behind, ahead)
        weight_on(kind, full, behind, partner)
        weight_in(kind, full, ahead)
        weight_on(kind, full, ahead, partner)

    for kind, _, full in stages:
        weight_in(kind, full, across)
        weight_on(kind, full, across, partner)
    def weights_whole(kind, src, full):
        pltpu.make_async_copy(src, full.at[owner_rows(dp)], w_own.at[kind]).wait()
        for k in range(NX):
            weight_in(kind, full, (chip + k) % NX * 2 + 1 - core)

    for stage in stages[:2]:
        weights_whole(*stage)

    arrived(X)
    to_rows(got.at[X], rows_x)

    def forward(n, _):
        gate = jnp.dot(rows_x[...], w_gate[:, cols(n)], preferred_element_type=f32)
        up = jnp.dot(rows_x[...], w_up[:, cols(n)], preferred_element_type=f32)
        sigma = jax.nn.sigmoid(gate)
        activated = gate * sigma
        act[:, cols(n)] = activated
        slope[:, cols(n)] = up * sigma * (1.0 + gate * (1.0 - sigma))
        hidden[:, cols(n)] = (activated * up).astype(bf16)
        return 0

    lax.fori_loop(0, ff // WIDE, forward, 0)
    across_ff = (((1,), (1,)), ((), ()))
    weights_whole(*stages[2])

    def project(n, _):
        rows_tmp[:, cols(n)] = lax.dot_general(
            hidden[...], w_down[cols(n), :], across_ff, preferred_element_type=f32
        ).astype(bf16)
        return 0

    lax.fori_loop(0, width // WIDE, project, 0)
    to_tiles(rows_tmp, sent.at[Y])
    exchange(Y)

    arrived(DY)
    to_rows(got.at[DY], rows_dy)

    def backward(n, _):
        d_hidden = jnp.dot(rows_dy[...], w_down[:, cols(n)], preferred_element_type=f32)
        d_gate[:, cols(n)] = (d_hidden * slope[:, cols(n)]).astype(bf16)
        d_up[:, cols(n)] = (d_hidden * act[:, cols(n)]).astype(bf16)
        return 0

    lax.fori_loop(0, ff // WIDE, backward, 0)

    def project_back(n, _):
        rows_tmp[:, cols(n)] = (
            lax.dot_general(d_gate[...], w_gate[cols(n), :], across_ff, preferred_element_type=f32)
            + lax.dot_general(d_up[...], w_up[cols(n), :], across_ff, preferred_element_type=f32)
        ).astype(bf16)
        return 0

    lax.fori_loop(0, width // WIDE, project_back, 0)
    to_tiles(rows_tmp, sent.at[DX])
    exchange(DX)

    def outer(n, _):
        part[cols(n), :] = lax.dot_general(
            rows_dy[:, cols(n)], hidden[...], (((0,), (0,)), ((), ())), preferred_element_type=f32
        ).astype(bf16)
        return 0

    lax.fori_loop(0, width // WIDE, outer, 0)
    pltpu.make_async_copy(part.at[owner_rows(dp)], parts.at[owner_rows(dp)], own_sem.at[4]).start()
    for k in range(1, n_dp):
        peer = (dp + k) % n_dp
        pltpu.make_async_remote_copy(
            part.at[owner_rows(peer)],
            parts.at[owner_rows(dp)],
            p_send,
            p_recv,
            device_id=(peer, e),
            device_id_type=MESH,
        ).start()

    token_col = lax.broadcasted_iota(jnp.int32, (tok, rows), 1)
    home0 = jnp.where(token_col == column(row_of[0]), 1.0, 0.0).astype(bf16)
    home1 = jnp.where(token_col == column(row_of[1]), 1.0, 0.0).astype(bf16)

    gate0, gate1 = column(gates_ref[0:1, :]), column(gates_ref[1:2, :])

    arrived(Y)
    to_rows(got.at[Y], rows_tmp)

    def combine(n, _):
        first = jnp.dot(home0, rows_tmp[:, cols(n)], preferred_element_type=f32)
        second = jnp.dot(home1, rows_tmp[:, cols(n)], preferred_element_type=f32)
        moe_ref[:, cols(n)] = (
            gate0 * first + gate1 * second
        ).astype(bf16)
        return 0

    lax.fori_loop(0, width // WIDE, combine, 0)

    others = pl.ds(0, (n_dp - 1) * shard)
    pltpu.make_async_remote_copy(
        part.at[others], parts.at[others], p_send, p_recv, device_id=(partner, e), device_id_type=MESH
    ).wait_recv()
    pltpu.make_async_copy(part.at[owner_rows(dp)], parts.at[owner_rows(dp)], own_sem.at[4]).wait()

    def total(n, _):
        acc = None
        for p in range(n_dp):
            r = pl.ds(pl.multiple_of(p * shard + n * 32, 32), 32)
            term = parts[r, :].astype(f32)
            acc = term if acc is None else acc + term
        dgrad_ref[pl.ds(pl.multiple_of(n * 32, 32), 32), :] = acc.astype(bf16)
        return 0

    lax.fori_loop(0, shard // 32, total, 0)

    arrived(DX)
    to_rows(got.at[DX], rows_tmp, True)
    home = home0 + home1

    def collect(n, _):
        tgrad_ref[:, cols(n)] = jnp.dot(
            home, rows_tmp[:, cols(n)], preferred_element_type=f32
        ).astype(bf16)
        return 0

    lax.fori_loop(0, width // WIDE, collect, 0, unroll=True)

    for ph in range(4):
        drained(ph)
    for kind, src, full in stages:
        own3, on4 = pl.ds(0, 3 * shard), pl.ds(0, 4 * shard)
        pltpu.make_async_remote_copy(
            full.at[own3], full.at[own3], w_send.at[kind], w_recv.at[kind, dp],
            device_id=(partner, e), device_id_type=MESH,
        ).wait_send()
        pltpu.make_async_remote_copy(
            full.at[on4], full.at[on4], w_pass.at[kind], w_recv.at[kind, dp],
            device_id=(partner, e), device_id_type=MESH,
        ).wait_send()
    pltpu.make_async_remote_copy(
        part.at[others], parts.at[others], p_send, p_recv, device_id=(partner, e), device_id_type=MESH
    ).wait_send()


def put(*refs):
    n = len(refs) // 2
    copies = [pltpu.make_async_copy(refs[i], refs[n + i], refs[2 * n].at[i]) for i in range(n)]
    for copy in copies:
        copy.start()
    for copy in copies:
        copy.wait()


def put_out(*arrays):
    n = len(arrays)
    return pl.pallas_call(
        put,
        out_shape=[jax.ShapeDtypeStruct(a.shape, a.dtype) for a in arrays],
        in_specs=[pl.BlockSpec(memory_space=pltpu.VMEM)] * n,
        out_specs=[pl.BlockSpec(memory_space=pl.ANY)] * n,
        scratch_shapes=[pltpu.SemaphoreType.DMA((n,))],
        name="put_out",
    )(*[pltpu.with_memory_space_constraint(a, pltpu.VMEM) for a in arrays])


def per_device(tokens, out_grad, route_gates, route_slot, gate_weight, up_weight, down_weight):
    tok_dev, width = tokens.shape
    top = route_slot.shape[1]
    n_exp = lax.axis_size("expert")
    n_dp = lax.axis_size("dp")
    cap = max(2, (5 * tok_dev * top + 4 * n_exp - 1) // (4 * n_exp))
    rows = n_exp * cap
    ff = gate_weight.shape[2]
    shard = width // n_dp
    bf16, f32 = jnp.bfloat16, jnp.float32
    vmem = pl.BlockSpec(memory_space=pltpu.VMEM)
    away = pl.BlockSpec(memory_space=pl.ANY)
    dma = pltpu.SemaphoreType.DMA
    flat = rows * SUB
    moe, tgrad, dgrad = pl.pallas_call(
        functools.partial(layer, cap),
        out_shape=(
            pltpu.VMEM((tok_dev, width), bf16),
            pltpu.VMEM((tok_dev, width), bf16),
            pltpu.VMEM((shard, ff), bf16),
        ),
        in_specs=[vmem] * 4 + [away] * 3,
        out_specs=(vmem, vmem, vmem),
        scratch_shapes=[
            pltpu.VMEM((WIDE, WIDE), bf16),
            pltpu.VMEM((width, ff), bf16),
            pltpu.VMEM((width, ff), bf16),
            pltpu.VMEM((width, ff), bf16),
            pltpu.VMEM((4, flat, LANES), bf16),
            pltpu.VMEM((4, flat, LANES), bf16),
            pltpu.VMEM((rows, width), bf16),
            pltpu.VMEM((rows, width), bf16),
            pltpu.VMEM((rows, width), bf16),
            pltpu.VMEM((rows, ff), f32),
            pltpu.VMEM((rows, ff), f32),
            pltpu.VMEM((rows, ff), bf16),
            pltpu.VMEM((rows, ff), bf16),
            pltpu.VMEM((rows, ff), bf16),
            pltpu.VMEM((width, ff), bf16),
            pltpu.VMEM((width, ff), bf16),
            dma((4,)),
            dma((4,)),
            dma((5,)),
            dma((3,)),
            dma((3,)),
            dma((3,)),
            dma((3, n_dp)),
            dma,
            dma,
            pltpu.SemaphoreType.REGULAR((2,)),
        ],
        name="expert_layer",
        compiler_params=pltpu.CompilerParams(
            collective_id=0, has_side_effects=True, vmem_limit_bytes=60 * 1024 * 1024
        ),
    )(
        route_slot.T,
        route_gates.T,
        tokens,
        out_grad,
        gate_weight[0],
        up_weight[0],
        down_weight[0],
    )
    moe, tgrad, dgrad = put_out(moe, tgrad, dgrad)
    return moe, tgrad, dgrad[None]


def solution(mesh):
    rows = P(("dp", "expert"), None)
    weights = P("expert", "dp", None)
    return jax.shard_map(
        per_device,
        mesh=mesh,
        in_specs=(rows, rows, rows, rows, weights, weights, weights),
        out_specs=(rows, rows, weights),
        check_vma=False,
    )
```

```python
import functools

import jax
import jax.numpy as jnp
from jax import lax
from jax.experimental import pallas as pl
from jax.experimental.pallas import tpu as pltpu
from jax.sharding import PartitionSpec as P

LANES = 128
SUB = 16
NX, NY, NZ = 4, 4, 16
WIDE = 256
MESH = pl.DeviceIdType.MESH
X, DY, Y, DX = range(4)


def layer(
    cap,
    slots_ref,
    gates_ref,
    tokens_ref,
    grads_ref,
    gate_in,
    up_in,
    down_in,
    moe_ref,
    tgrad_ref,
    dgrad_ref,
    perm,
    w_gate,
    w_up,
    w_down,
    sent,
    got,
    rows_x,
    rows_dy,
    rows_tmp,
    slope,
    act,
    hidden,
    d_gate,
    d_up,
    part,
    parts,
    partial,
    send_sem,
    recv_sem,
    own_sem,
    w_own,
    w_send,
    w_pass,
    w_recv,
    p_send,
    p_recv,
    near,
):
    f32, bf16 = jnp.float32, jnp.bfloat16
    dp, e = lax.axis_index("dp"), lax.axis_index("expert")
    y, z = e // NZ, e % NZ
    chip, core = dp // 2, dp % 2
    n_exp, n_dp = NY * NZ, NX * 2
    rows = n_exp * cap
    width = tokens_ref.shape[1]
    shard = width // n_dp
    ff = hidden.shape[1]
    unit = cap * SUB

    barrier = pltpu.get_barrier_semaphore()

    above = y * NZ + (z + 1) % NZ
    below = y * NZ + (z + NZ - 1) % NZ
    for a in range(1, NY):
        pl.semaphore_signal(
            barrier, inc=1, device_id=(dp, (y + a) % NY * NZ + z), device_id_type=MESH
        )
    for p in (above, below):
        pl.semaphore_signal(barrier, inc=1, device_id=(dp, p), device_id_type=MESH)
    for k in range(1, n_dp):
        pl.semaphore_signal(barrier, inc=1, device_id=((dp + k) % n_dp, e), device_id_type=MESH)

    def tell():
        pl.semaphore_signal(near.at[0], inc=1, device_id=(dp, above), device_id_type=MESH)
        pl.semaphore_signal(near.at[1], inc=1, device_id=(dp, below), device_id_type=MESH)

    def meet():
        pl.semaphore_wait(near.at[0], 1)
        pl.semaphore_wait(near.at[1], 1)

    def block(p):
        return pl.ds(pl.multiple_of(p * unit, SUB), unit)

    def owner_rows(p):
        return pl.ds(pl.multiple_of(p * shard, shard), shard)

    def cols(n):
        return pl.ds(pl.multiple_of(n * WIDE, WIDE), WIDE)

    at = lax.broadcasted_iota(jnp.int32, (WIDE, WIDE), 0)
    to = lax.broadcasted_iota(jnp.int32, (WIDE, WIDE), 1)
    perm[...] = jnp.where((at % SUB) * SUB + at // SUB == to, 1.0, 0.0).astype(bf16)

    def to_tiles(nat, flat, first=0, last=rows // 32, unroll=False):
        def step(g, _):
            halves = []
            for h in range(2):
                r = pl.ds(pl.multiple_of(g * 32 + h * SUB, SUB), SUB)
                halves.append(
                    jnp.concatenate(
                        [nat[r, j * LANES : (j + 1) * LANES] for j in range(SUB)], axis=0
                    )
                )
            moved = jnp.dot(
                perm[...], jnp.concatenate(halves, axis=1), preferred_element_type=f32
            ).astype(bf16)
            for h in range(2):
                r = pl.ds(pl.multiple_of(g * 512 + h * WIDE, WIDE), WIDE)
                flat[r, :] = moved[:, h * LANES : (h + 1) * LANES]
            return 0

        lax.fori_loop(first, last, step, 0, unroll=unroll)

    def to_rows(flat, nat, unroll=False):
        def step(g, _):
            halves = [
                flat[pl.ds(pl.multiple_of(g * 512 + h * WIDE, WIDE), WIDE), :] for h in range(2)
            ]
            moved = jnp.dot(
                perm[...], jnp.concatenate(halves, axis=1), preferred_element_type=f32
            ).astype(bf16)
            for h in range(2):
                r = pl.ds(pl.multiple_of(g * 32 + h * SUB, SUB), SUB)
                for j in range(SUB):
                    nat[r, j * LANES : (j + 1) * LANES] = moved[
                        j * SUB : (j + 1) * SUB, h * LANES : (h + 1) * LANES
                    ]
            return 0

        lax.fori_loop(0, rows // 32, step, 0, unroll=unroll)

    def send(ph, p, sem=None):
        sem = ph if sem is None else sem
        pltpu.make_async_remote_copy(
            sent.at[ph, block(p)],
            got.at[ph, block(e)],
            send_sem.at[sem],
            recv_sem.at[sem],
            device_id=(dp, p),
            device_id_type=MESH,
        ).start()

    def exchange(ph):
        pltpu.make_async_copy(
            sent.at[ph, block(e)], got.at[ph, block(e)], own_sem.at[ph]
        ).start()
        for a in range(1, NY):
            send(ph, (y + a) % NY * NZ + z)

        def step(i, _):
            for a in range(NY):
                send(ph, (y + a) % NY * NZ + (z + i) % NZ)
            return 0

        lax.fori_loop(1, NZ, step, 0)

    next_e = y * NZ + (z + 1) % NZ

    def arrived(ph):
        most = pl.ds(0, (n_exp - 1) * unit)
        pltpu.make_async_remote_copy(
            sent.at[ph, most],
            got.at[ph, most],
            send_sem.at[ph],
            recv_sem.at[ph],
            device_id=(dp, next_e),
            device_id_type=MESH,
        ).wait_recv()
        pltpu.make_async_copy(
            sent.at[ph, block(e)], got.at[ph, block(e)], own_sem.at[ph]
        ).wait()

    def drained(ph):
        most = pl.ds(0, (n_exp - 1) * unit)
        pltpu.make_async_remote_copy(
            sent.at[ph, most],
            got.at[ph, most],
            send_sem.at[ph],
            recv_sem.at[ph],
            device_id=(dp, next_e),
            device_id_type=MESH,
        ).wait_send()

    tok = tokens_ref.shape[0]
    down_to = lax.broadcasted_iota(jnp.int32, (tok, tok), 0)
    across_to = lax.broadcasted_iota(jnp.int32, (tok, tok), 1)

    def column(line):
        return jnp.sum(
            jnp.where(down_to == across_to, line, jnp.zeros_like(line)), axis=1, keepdims=True
        )

    lines = [slots_ref[k : k + 1, :] for k in range(2)]
    columns = [column(line) for line in lines]
    row_of = []
    for line in lines:
        same = (columns[0] == line) | (columns[1] == line)
        rank = jnp.sum(
            jnp.where(same & (down_to < across_to), 1, 0).astype(jnp.int32), axis=0, keepdims=True
        )
        row_of.append(line * cap + rank)

    slot_row = lax.broadcasted_iota(jnp.int32, (rows, tok), 0)
    hit0 = slot_row == row_of[0]
    hit1 = slot_row == row_of[1]
    pick = jnp.where(hit0 | hit1, 1.0, 0.0).astype(bf16)

    half = rows // 2

    def gather_x(h):
        held = pick[h * half : (h + 1) * half]

        def step(n, _):
            rows_tmp[h * half : (h + 1) * half, cols(n)] = jnp.dot(
                held, tokens_ref[:, cols(n)], preferred_element_type=f32
            ).astype(bf16)
            return 0

        lax.fori_loop(0, width // WIDE, step, 0, unroll=True)

    pl.semaphore_wait(barrier, NY - 1 + 2 + n_dp - 1)
    tell()
    def sides(k, lines):
        for to_y in lines:
            send(X, to_y * NZ + (z + k) % NZ)
            if k < NZ // 2:
                send(X, to_y * NZ + (z + NZ - k) % NZ)

    early, late = range(NY // 2), range(NY // 2, NY)
    gather_x(0)
    meet()
    tell()
    to_tiles(rows_tmp, sent.at[X], 0, rows // 64, True)
    sides(1, early)
    meet()
    tell()
    sides(2, early)
    gather_x(1)
    meet()
    tell()
    to_tiles(rows_tmp, sent.at[X], rows // 64, rows // 32, True)
    sides(1, late)
    sides(2, late)
    sides(3, range(NY))
    meet()
    tell()
    sides(4, range(NY))

    turn = 1 - 2 * core
    partner = chip * 2 + 1 - core
    ahead = (chip + NX + turn) % NX * 2 + core
    behind = (chip + NX - turn) % NX * 2 + core
    across = (chip + 2) % NX * 2 + core
    stages = ((0, gate_in, w_gate), (1, up_in, w_up), (2, down_in, w_down))
    for kind, src, full in stages:
        pltpu.make_async_copy(src, full.at[owner_rows(dp)], w_own.at[kind]).start()
        for peer in (ahead, behind, partner):
            pltpu.make_async_remote_copy(
                src,
                full.at[owner_rows(dp)],
                w_send.at[kind],
                w_recv.at[kind, dp],
                device_id=(peer, e),
                device_id_type=MESH,
            ).start()

    pltpu.make_async_copy(sent.at[X, block(e)], got.at[X, block(e)], own_sem.at[X]).start()
    for a in range(1, NY):
        send(X, (y + a) % NY * NZ + z)
    for k in range(5, NZ // 2 + 1):
        meet()
        if k < NZ // 2:
            tell()
        sides(k, range(NY))

    def weight_in(kind, full, owner):
        pltpu.make_async_remote_copy(
            full.at[owner_rows(owner)],
            full.at[owner_rows(owner)],
            w_pass.at[kind],
            w_recv.at[kind, owner],
            device_id=(partner, e),
            device_id_type=MESH,
        ).wait_recv()

    def weight_on(kind, full, owner, peer):
        pltpu.make_async_remote_copy(
            full.at[owner_rows(owner)],
            full.at[owner_rows(owner)],
            w_pass.at[kind],
            w_recv.at[kind, owner],
            device_id=(peer, e),
            device_id_type=MESH,
        ).start()

    share = jnp.sum(
        jnp.where(hit0, gates_ref[0:1, :], 0.0) + jnp.where(hit1, gates_ref[1:2, :], 0.0),
        axis=1,
        keepdims=True,
    )

    def gather_dy(n, _):
        taken = jnp.dot(pick, grads_ref[:, cols(n)], preferred_element_type=f32)
        rows_tmp[:, cols(n)] = (share * taken).astype(bf16)
        return 0

    lax.fori_loop(0, width // WIDE, gather_dy, 0)
    to_tiles(rows_tmp, sent.at[DY])
    exchange(DY)

    for kind, _, full in stages:
        weight_in(kind, full, behind)
        weight_on(kind, full, behind, ahead)
        weight_on(kind, full, behind, partner)
        weight_in(kind, full, ahead)
        weight_on(kind, full, ahead, partner)

    for kind, _, full in stages:
        weight_in(kind, full, across)
        weight_on(kind, full, across, partner)
    for kind, src, full in stages:
        pltpu.make_async_copy(src, full.at[owner_rows(dp)], w_own.at[kind]).wait()
        for k in range(NX):
            weight_in(kind, full, (chip + k) % NX * 2 + 1 - core)

    arrived(X)
    to_rows(got.at[X], rows_x)

    def forward(n, _):
        gate = jnp.dot(rows_x[...], w_gate[:, cols(n)], preferred_element_type=f32)
        up = jnp.dot(rows_x[...], w_up[:, cols(n)], preferred_element_type=f32)
        sigma = jax.nn.sigmoid(gate)
        activated = gate * sigma
        act[:, cols(n)] = activated
        slope[:, cols(n)] = up * sigma * (1.0 + gate * (1.0 - sigma))
        hidden[:, cols(n)] = (activated * up).astype(bf16)
        return 0

    lax.fori_loop(0, ff // WIDE, forward, 0)
    across_ff = (((1,), (1,)), ((), ()))

    def project(n, _):
        rows_tmp[:, cols(n)] = lax.dot_general(
            hidden[...], w_down[cols(n), :], across_ff, preferred_element_type=f32
        ).astype(bf16)
        return 0

    lax.fori_loop(0, width // WIDE, project, 0)
    to_tiles(rows_tmp, sent.at[Y])
    exchange(Y)

    arrived(DY)
    to_rows(got.at[DY], rows_dy)

    def backward(n, _):
        d_hidden = jnp.dot(rows_dy[...], w_down[:, cols(n)], preferred_element_type=f32)
        d_gate[:, cols(n)] = (d_hidden * slope[:, cols(n)]).astype(bf16)
        d_up[:, cols(n)] = (d_hidden * act[:, cols(n)]).astype(bf16)
        return 0

    lax.fori_loop(0, ff // WIDE, backward, 0)

    def project_back(n, _):
        rows_tmp[:, cols(n)] = (
            lax.dot_general(d_gate[...], w_gate[cols(n), :], across_ff, preferred_element_type=f32)
            + lax.dot_general(d_up[...], w_up[cols(n), :], across_ff, preferred_element_type=f32)
        ).astype(bf16)
        return 0

    lax.fori_loop(0, width // WIDE, project_back, 0)
    to_tiles(rows_tmp, sent.at[DX])
    pair, other = y // 2, 1 - y // 2
    pltpu.make_async_copy(sent.at[DX, block(e)], got.at[DX, block(e)], own_sem.at[DX]).start()
    beside = pair * 2 + 1 - y % 2

    def send_near(i, _):
        for to_y in (y, beside):
            send(DX, to_y * NZ + (z + i) % NZ)
        return 0

    def send_other(i, _):
        for k in range(2):
            send(DX, (other * 2 + k) * NZ + (z + i) % NZ, 4)
        return 0

    send(DX, beside * NZ + z)
    lax.fori_loop(1, NZ, send_near, 0)
    lax.fori_loop(0, NZ, send_other, 0)

    def outer(n, _):
        part[cols(n), :] = lax.dot_general(
            rows_dy[:, cols(n)], hidden[...], (((0,), (0,)), ((), ())), preferred_element_type=f32
        ).astype(bf16)
        return 0

    lax.fori_loop(0, width // WIDE, outer, 0)
    pltpu.make_async_copy(part.at[owner_rows(dp)], parts.at[owner_rows(dp)], own_sem.at[4]).start()
    for k in range(1, n_dp):
        peer = (dp + k) % n_dp
        pltpu.make_async_remote_copy(
            part.at[owner_rows(peer)],
            parts.at[owner_rows(dp)],
            p_send,
            p_recv,
            device_id=(peer, e),
            device_id_type=MESH,
        ).start()

    token_col = lax.broadcasted_iota(jnp.int32, (tok, rows), 1)
    home0 = jnp.where(token_col == column(row_of[0]), 1.0, 0.0).astype(bf16)
    home1 = jnp.where(token_col == column(row_of[1]), 1.0, 0.0).astype(bf16)

    gate0, gate1 = column(gates_ref[0:1, :]), column(gates_ref[1:2, :])

    arrived(Y)
    to_rows(got.at[Y], rows_tmp)

    def combine(n, _):
        first = jnp.dot(home0, rows_tmp[:, cols(n)], preferred_element_type=f32)
        second = jnp.dot(home1, rows_tmp[:, cols(n)], preferred_element_type=f32)
        moe_ref[:, cols(n)] = (
            gate0 * first + gate1 * second
        ).astype(bf16)
        return 0

    lax.fori_loop(0, width // WIDE, combine, 0)

    others = pl.ds(0, (n_dp - 1) * shard)
    pltpu.make_async_remote_copy(
        part.at[others], parts.at[others], p_send, p_recv, device_id=(partner, e), device_id_type=MESH
    ).wait_recv()
    pltpu.make_async_copy(part.at[owner_rows(dp)], parts.at[owner_rows(dp)], own_sem.at[4]).wait()

    def total(n, _):
        acc = None
        for p in range(n_dp):
            r = pl.ds(pl.multiple_of(p * shard + n * 32, 32), 32)
            term = parts[r, :].astype(f32)
            acc = term if acc is None else acc + term
        dgrad_ref[pl.ds(pl.multiple_of(n * 32, 32), 32), :] = acc.astype(bf16)
        return 0

    lax.fori_loop(0, shard // 32, total, 0)

    pair_rows = NZ * 2 * unit

    def half_dx(count, sem):
        some = pl.ds(0, count * unit)
        return pltpu.make_async_remote_copy(
            sent.at[DX, some],
            got.at[DX, some],
            send_sem.at[sem],
            recv_sem.at[sem],
            device_id=(dp, next_e),
            device_id_type=MESH,
        )

    col_half = lax.broadcasted_iota(jnp.int32, (tok, half), 1)

    def home_of(which):
        at_row = col_half + which * half
        mine = (at_row == column(row_of[0])) | (at_row == column(row_of[1]))
        return jnp.where(mine, 1.0, 0.0).astype(bf16)

    def pair_in(which):
        def step(g, _):
            halves = [
                got[
                    DX,
                    pl.ds(pl.multiple_of(which * pair_rows + g * 512 + h * WIDE, WIDE), WIDE),
                    :,
                ]
                for h in range(2)
            ]
            moved = jnp.dot(
                perm[...], jnp.concatenate(halves, axis=1), preferred_element_type=f32
            ).astype(bf16)
            for h in range(2):
                for j in range(SUB):
                    rows_tmp[
                        g * 32 + h * SUB : g * 32 + (h + 1) * SUB, j * LANES : (j + 1) * LANES
                    ] = moved[j * SUB : (j + 1) * SUB, h * LANES : (h + 1) * LANES]
            return 0

        for g in range(rows // 64):
            step(g, 0)

    home_pair, home_other = home_of(pair), home_of(other)
    half_dx(NZ * 2 - 1, DX).wait_recv()
    pltpu.make_async_copy(sent.at[DX, block(e)], got.at[DX, block(e)], own_sem.at[DX]).wait()
    pair_in(pair)
    for n in range(width // WIDE):
        c = slice(n * WIDE, (n + 1) * WIDE)
        partial[:, c] = jnp.dot(home_pair, rows_tmp[0:half, c], preferred_element_type=f32)
    half_dx(NZ * 2, 4).wait_recv()
    pair_in(other)
    for n in range(width // WIDE):
        c = slice(n * WIDE, (n + 1) * WIDE)
        tgrad_ref[:, c] = (
            partial[:, c] + jnp.dot(home_other, rows_tmp[0:half, c], preferred_element_type=f32)
        ).astype(bf16)

    half_dx(NZ * 2 - 1, DX).wait_send()
    half_dx(NZ * 2, 4).wait_send()
    for ph in range(3):
        drained(ph)
    for kind, src, full in stages:
        own3, on4 = pl.ds(0, 3 * shard), pl.ds(0, 4 * shard)
        pltpu.make_async_remote_copy(
            full.at[own3], full.at[own3], w_send.at[kind], w_recv.at[kind, dp],
            device_id=(partner, e), device_id_type=MESH,
        ).wait_send()
        pltpu.make_async_remote_copy(
            full.at[on4], full.at[on4], w_pass.at[kind], w_recv.at[kind, dp],
            device_id=(partner, e), device_id_type=MESH,
        ).wait_send()
    pltpu.make_async_remote_copy(
        part.at[others], parts.at[others], p_send, p_recv, device_id=(partner, e), device_id_type=MESH
    ).wait_send()


def put(*refs):
    n = len(refs) // 2
    copies = [pltpu.make_async_copy(refs[i], refs[n + i], refs[2 * n].at[i]) for i in range(n)]
    for copy in copies:
        copy.start()
    for copy in copies:
        copy.wait()


def put_out(*arrays):
    n = len(arrays)
    return pl.pallas_call(
        put,
        out_shape=[jax.ShapeDtypeStruct(a.shape, a.dtype) for a in arrays],
        in_specs=[pl.BlockSpec(memory_space=pltpu.VMEM)] * n,
        out_specs=[pl.BlockSpec(memory_space=pl.ANY)] * n,
        scratch_shapes=[pltpu.SemaphoreType.DMA((n,))],
        name="put_out",
    )(*[pltpu.with_memory_space_constraint(a, pltpu.VMEM) for a in arrays])


def per_device(tokens, out_grad, route_gates, route_slot, gate_weight, up_weight, down_weight):
    tok_dev, width = tokens.shape
    top = route_slot.shape[1]
    n_exp = lax.axis_size("expert")
    n_dp = lax.axis_size("dp")
    cap = max(2, (5 * tok_dev * top + 4 * n_exp - 1) // (4 * n_exp))
    rows = n_exp * cap
    ff = gate_weight.shape[2]
    shard = width // n_dp
    bf16, f32 = jnp.bfloat16, jnp.float32
    vmem = pl.BlockSpec(memory_space=pltpu.VMEM)
    away = pl.BlockSpec(memory_space=pl.ANY)
    dma = pltpu.SemaphoreType.DMA
    flat = rows * SUB
    moe, tgrad, dgrad = pl.pallas_call(
        functools.partial(layer, cap),
        out_shape=(
            pltpu.VMEM((tok_dev, width), bf16),
            pltpu.VMEM((tok_dev, width), bf16),
            pltpu.VMEM((shard, ff), bf16),
        ),
        in_specs=[vmem] * 4 + [away] * 3,
        out_specs=(vmem, vmem, vmem),
        scratch_shapes=[
            pltpu.VMEM((WIDE, WIDE), bf16),
            pltpu.VMEM((width, ff), bf16),
            pltpu.VMEM((width, ff), bf16),
            pltpu.VMEM((width, ff), bf16),
            pltpu.VMEM((4, flat, LANES), bf16),
            pltpu.VMEM((4, flat, LANES), bf16),
            pltpu.VMEM((rows, width), bf16),
            pltpu.VMEM((rows, width), bf16),
            pltpu.VMEM((rows, width), bf16),
            pltpu.VMEM((rows, ff), f32),
            pltpu.VMEM((rows, ff), f32),
            pltpu.VMEM((rows, ff), bf16),
            pltpu.VMEM((rows, ff), bf16),
            pltpu.VMEM((rows, ff), bf16),
            pltpu.VMEM((width, ff), bf16),
            pltpu.VMEM((width, ff), bf16),
            pltpu.VMEM((tok_dev, width), f32),
            dma((5,)),
            dma((5,)),
            dma((5,)),
            dma((3,)),
            dma((3,)),
            dma((3,)),
            dma((3, n_dp)),
            dma,
            dma,
            pltpu.SemaphoreType.REGULAR((2,)),
        ],
        name="expert_layer",
        compiler_params=pltpu.CompilerParams(
            collective_id=0, has_side_effects=True, vmem_limit_bytes=60 * 1024 * 1024
        ),
    )(
        route_slot.T,
        route_gates.T,
        tokens,
        out_grad,
        gate_weight[0],
        up_weight[0],
        down_weight[0],
    )
    moe, tgrad, dgrad = put_out(moe, tgrad, dgrad)
    return moe, tgrad, dgrad[None]


def solution(mesh):
    rows = P(("dp", "expert"), None)
    weights = P("expert", "dp", None)
    return jax.shard_map(
        per_device,
        mesh=mesh,
        in_specs=(rows, rows, rows, rows, weights, weights, weights),
        out_specs=(rows, rows, weights),
        check_vma=False,
    )
```

```python
import functools

import jax
import jax.numpy as jnp
from jax import lax
from jax.experimental import pallas as pl
from jax.experimental.pallas import tpu as pltpu
from jax.sharding import PartitionSpec as P

LANES = 128
SUB = 16
NX, NY, NZ = 4, 4, 16
WIDE = 256
MESH = pl.DeviceIdType.MESH
X, DY, Y, DX = range(4)


def layer(
    cap,
    slots_ref,
    gates_ref,
    tokens_ref,
    grads_ref,
    gate_in,
    up_in,
    down_in,
    moe_ref,
    tgrad_ref,
    dgrad_ref,
    perm,
    w_gate,
    w_up,
    w_down,
    sent,
    got,
    rows_x,
    rows_dy,
    rows_tmp,
    slope,
    act,
    hidden,
    d_gate,
    d_up,
    part,
    parts,
    send_sem,
    recv_sem,
    own_sem,
    w_own,
    w_send,
    w_pass,
    w_recv,
    p_send,
    p_recv,
    near,
):
    f32, bf16 = jnp.float32, jnp.bfloat16
    dp, e = lax.axis_index("dp"), lax.axis_index("expert")
    y, z = e // NZ, e % NZ
    chip, core = dp // 2, dp % 2
    n_exp, n_dp = NY * NZ, NX * 2
    rows = n_exp * cap
    width = tokens_ref.shape[1]
    shard = width // n_dp
    ff = hidden.shape[1]
    unit = cap * SUB

    barrier = pltpu.get_barrier_semaphore()

    above = y * NZ + (z + 1) % NZ
    below = y * NZ + (z + NZ - 1) % NZ
    for a in range(1, NY):
        pl.semaphore_signal(
            barrier, inc=1, device_id=(dp, (y + a) % NY * NZ + z), device_id_type=MESH
        )
    for p in (above, below):
        pl.semaphore_signal(barrier, inc=1, device_id=(dp, p), device_id_type=MESH)
    for k in range(1, n_dp):
        pl.semaphore_signal(barrier, inc=1, device_id=((dp + k) % n_dp, e), device_id_type=MESH)

    def tell():
        pl.semaphore_signal(near.at[0], inc=1, device_id=(dp, above), device_id_type=MESH)
        pl.semaphore_signal(near.at[1], inc=1, device_id=(dp, below), device_id_type=MESH)

    def meet():
        pl.semaphore_wait(near.at[0], 1)
        pl.semaphore_wait(near.at[1], 1)

    def block(p):
        return pl.ds(pl.multiple_of(p * unit, SUB), unit)

    def owner_rows(p):
        return pl.ds(pl.multiple_of(p * shard, shard), shard)

    def cols(n):
        return pl.ds(pl.multiple_of(n * WIDE, WIDE), WIDE)

    at = lax.broadcasted_iota(jnp.int32, (WIDE, WIDE), 0)
    to = lax.broadcasted_iota(jnp.int32, (WIDE, WIDE), 1)
    perm[...] = jnp.where((at % SUB) * SUB + at // SUB == to, 1.0, 0.0).astype(bf16)

    def to_tiles(nat, flat, first=0, last=rows // 32, unroll=False):
        def step(g, _):
            halves = []
            for h in range(2):
                r = pl.ds(pl.multiple_of(g * 32 + h * SUB, SUB), SUB)
                halves.append(
                    jnp.concatenate(
                        [nat[r, j * LANES : (j + 1) * LANES] for j in range(SUB)], axis=0
                    )
                )
            moved = jnp.dot(
                perm[...], jnp.concatenate(halves, axis=1), preferred_element_type=f32
            ).astype(bf16)
            for h in range(2):
                r = pl.ds(pl.multiple_of(g * 512 + h * WIDE, WIDE), WIDE)
                flat[r, :] = moved[:, h * LANES : (h + 1) * LANES]
            return 0

        lax.fori_loop(first, last, step, 0, unroll=unroll)

    def to_rows(flat, nat, unroll=False):
        def step(g, _):
            halves = [
                flat[pl.ds(pl.multiple_of(g * 512 + h * WIDE, WIDE), WIDE), :] for h in range(2)
            ]
            moved = jnp.dot(
                perm[...], jnp.concatenate(halves, axis=1), preferred_element_type=f32
            ).astype(bf16)
            for h in range(2):
                r = pl.ds(pl.multiple_of(g * 32 + h * SUB, SUB), SUB)
                for j in range(SUB):
                    nat[r, j * LANES : (j + 1) * LANES] = moved[
                        j * SUB : (j + 1) * SUB, h * LANES : (h + 1) * LANES
                    ]
            return 0

        lax.fori_loop(0, rows // 32, step, 0, unroll=unroll)

    def send(ph, p):
        pltpu.make_async_remote_copy(
            sent.at[ph, block(p)],
            got.at[ph, block(e)],
            send_sem.at[ph],
            recv_sem.at[ph],
            device_id=(dp, p),
            device_id_type=MESH,
        ).start()

    def exchange(ph):
        pltpu.make_async_copy(
            sent.at[ph, block(e)], got.at[ph, block(e)], own_sem.at[ph]
        ).start()
        for a in range(1, NY):
            send(ph, (y + a) % NY * NZ + z)

        def step(i, _):
            for a in range(NY):
                send(ph, (y + a) % NY * NZ + (z + i) % NZ)
            return 0

        lax.fori_loop(1, NZ, step, 0)

    next_e = y * NZ + (z + 1) % NZ

    def arrived(ph):
        most = pl.ds(0, (n_exp - 1) * unit)
        pltpu.make_async_remote_copy(
            sent.at[ph, most],
            got.at[ph, most],
            send_sem.at[ph],
            recv_sem.at[ph],
            device_id=(dp, next_e),
            device_id_type=MESH,
        ).wait_recv()
        pltpu.make_async_copy(
            sent.at[ph, block(e)], got.at[ph, block(e)], own_sem.at[ph]
        ).wait()

    def drained(ph):
        most = pl.ds(0, (n_exp - 1) * unit)
        pltpu.make_async_remote_copy(
            sent.at[ph, most],
            got.at[ph, most],
            send_sem.at[ph],
            recv_sem.at[ph],
            device_id=(dp, next_e),
            device_id_type=MESH,
        ).wait_send()

    tok = tokens_ref.shape[0]
    down_to = lax.broadcasted_iota(jnp.int32, (tok, tok), 0)
    across_to = lax.broadcasted_iota(jnp.int32, (tok, tok), 1)

    def column(line):
        return jnp.sum(
            jnp.where(down_to == across_to, line, jnp.zeros_like(line)), axis=1, keepdims=True
        )

    lines = [slots_ref[k : k + 1, :] for k in range(2)]
    columns = [column(line) for line in lines]
    row_of = []
    for line in lines:
        same = (columns[0] == line) | (columns[1] == line)
        rank = jnp.sum(
            jnp.where(same & (down_to < across_to), 1, 0).astype(jnp.int32), axis=0, keepdims=True
        )
        row_of.append(line * cap + rank)

    slot_row = lax.broadcasted_iota(jnp.int32, (rows, tok), 0)
    hit0 = slot_row == row_of[0]
    hit1 = slot_row == row_of[1]
    pick = jnp.where(hit0 | hit1, 1.0, 0.0).astype(bf16)

    def gather_x(n, _):
        rows_tmp[:, cols(n)] = jnp.dot(
            pick, tokens_ref[:, cols(n)], preferred_element_type=f32
        ).astype(bf16)
        return 0

    pl.semaphore_wait(barrier, NY - 1 + 2 + n_dp - 1)
    tell()
    lax.fori_loop(0, width // WIDE, gather_x, 0, unroll=True)
    meet()
    tell()
    to_tiles(rows_tmp, sent.at[X], 0, rows // 64, True)
    meet()
    tell()
    to_tiles(rows_tmp, sent.at[X], rows // 64, rows // 32, True)
    meet()
    tell()

    turn = 1 - 2 * core
    partner = chip * 2 + 1 - core
    ahead = (chip + NX + turn) % NX * 2 + core
    behind = (chip + NX - turn) % NX * 2 + core
    across = (chip + 2) % NX * 2 + core
    stages = ((0, gate_in, w_gate), (1, up_in, w_up), (2, down_in, w_down))
    pltpu.make_async_copy(sent.at[X, block(e)], got.at[X, block(e)], own_sem.at[X]).start()
    for a in range(1, NY):
        send(X, (y + a) % NY * NZ + z)
    for k in range(1, 4):
        for a in range(NY):
            send(X, (y + a) % NY * NZ + (z + k) % NZ)
            send(X, (y + a) % NY * NZ + (z + NZ - k) % NZ)

    for kind, src, full in stages:
        pltpu.make_async_copy(src, full.at[owner_rows(dp)], w_own.at[kind]).start()
        for peer in (ahead, behind, partner):
            pltpu.make_async_remote_copy(
                src,
                full.at[owner_rows(dp)],
                w_send.at[kind],
                w_recv.at[kind, dp],
                device_id=(peer, e),
                device_id_type=MESH,
            ).start()

    for k in range(4, NZ // 2 + 1):
        meet()
        if k < NZ // 2:
            tell()
        for a in range(NY):
            send(X, (y + a) % NY * NZ + (z + k) % NZ)
            if k < NZ // 2:
                send(X, (y + a) % NY * NZ + (z + NZ - k) % NZ)

    def weight_in(kind, full, owner):
        pltpu.make_async_remote_copy(
            full.at[owner_rows(owner)],
            full.at[owner_rows(owner)],
            w_pass.at[kind],
            w_recv.at[kind, owner],
            device_id=(partner, e),
            device_id_type=MESH,
        ).wait_recv()

    def weight_on(kind, full, owner, peer):
        pltpu.make_async_remote_copy(
            full.at[owner_rows(owner)],
            full.at[owner_rows(owner)],
            w_pass.at[kind],
            w_recv.at[kind, owner],
            device_id=(peer, e),
            device_id_type=MESH,
        ).start()

    share = jnp.sum(
        jnp.where(hit0, gates_ref[0:1, :], 0.0) + jnp.where(hit1, gates_ref[1:2, :], 0.0),
        axis=1,
        keepdims=True,
    )

    def gather_dy(n, _):
        taken = jnp.dot(pick, grads_ref[:, cols(n)], preferred_element_type=f32)
        rows_tmp[:, cols(n)] = (share * taken).astype(bf16)
        return 0

    lax.fori_loop(0, width // WIDE, gather_dy, 0)
    to_tiles(rows_tmp, sent.at[DY])
    exchange(DY)

    for kind, _, full in stages:
        weight_in(kind, full, behind)
        weight_on(kind, full, behind, ahead)
        weight_on(kind, full, behind, partner)
        weight_in(kind, full, ahead)
        weight_on(kind, full, ahead, partner)

    for kind, _, full in stages:
        weight_in(kind, full, across)
        weight_on(kind, full, across, partner)
    for kind, src, full in stages:
        pltpu.make_async_copy(src, full.at[owner_rows(dp)], w_own.at[kind]).wait()
        for k in range(NX):
            weight_in(kind, full, (chip + k) % NX * 2 + 1 - core)

    arrived(X)
    to_rows(got.at[X], rows_x)

    def forward(n, _):
        gate = jnp.dot(rows_x[...], w_gate[:, cols(n)], preferred_element_type=f32)
        up = jnp.dot(rows_x[...], w_up[:, cols(n)], preferred_element_type=f32)
        sigma = jax.nn.sigmoid(gate)
        activated = gate * sigma
        act[:, cols(n)] = activated
        slope[:, cols(n)] = up * sigma * (1.0 + gate * (1.0 - sigma))
        hidden[:, cols(n)] = (activated * up).astype(bf16)
        return 0

    lax.fori_loop(0, ff // WIDE, forward, 0)
    across_ff = (((1,), (1,)), ((), ()))

    def project(n, _):
        rows_tmp[:, cols(n)] = lax.dot_general(
            hidden[...], w_down[cols(n), :], across_ff, preferred_element_type=f32
        ).astype(bf16)
        return 0

    lax.fori_loop(0, width // WIDE, project, 0)
    to_tiles(rows_tmp, sent.at[Y])
    exchange(Y)

    arrived(DY)
    to_rows(got.at[DY], rows_dy)

    def backward(n, _):
        d_hidden = jnp.dot(rows_dy[...], w_down[:, cols(n)], preferred_element_type=f32)
        d_gate[:, cols(n)] = (d_hidden * slope[:, cols(n)]).astype(bf16)
        d_up[:, cols(n)] = (d_hidden * act[:, cols(n)]).astype(bf16)
        return 0

    lax.fori_loop(0, ff // WIDE, backward, 0)

    def project_back(n, _):
        rows_tmp[:, cols(n)] = (
            lax.dot_general(d_gate[...], w_gate[cols(n), :], across_ff, preferred_element_type=f32)
            + lax.dot_general(d_up[...], w_up[cols(n), :], across_ff, preferred_element_type=f32)
        ).astype(bf16)
        return 0

    lax.fori_loop(0, width // WIDE, project_back, 0)
    to_tiles(rows_tmp, sent.at[DX])
    exchange(DX)

    def outer(n, _):
        part[cols(n), :] = lax.dot_general(
            rows_dy[:, cols(n)], hidden[...], (((0,), (0,)), ((), ())), preferred_element_type=f32
        ).astype(bf16)
        return 0

    lax.fori_loop(0, width // WIDE, outer, 0)
    pltpu.make_async_copy(part.at[owner_rows(dp)], parts.at[owner_rows(dp)], own_sem.at[4]).start()
    for k in range(1, n_dp):
        peer = (dp + k) % n_dp
        pltpu.make_async_remote_copy(
            part.at[owner_rows(peer)],
            parts.at[owner_rows(dp)],
            p_send,
            p_recv,
            device_id=(peer, e),
            device_id_type=MESH,
        ).start()

    token_col = lax.broadcasted_iota(jnp.int32, (tok, rows), 1)
    home0 = jnp.where(token_col == column(row_of[0]), 1.0, 0.0).astype(bf16)
    home1 = jnp.where(token_col == column(row_of[1]), 1.0, 0.0).astype(bf16)

    gate0, gate1 = column(gates_ref[0:1, :]), column(gates_ref[1:2, :])

    arrived(Y)
    to_rows(got.at[Y], rows_tmp)

    def combine(n, _):
        first = jnp.dot(home0, rows_tmp[:, cols(n)], preferred_element_type=f32)
        second = jnp.dot(home1, rows_tmp[:, cols(n)], preferred_element_type=f32)
        moe_ref[:, cols(n)] = (
            gate0 * first + gate1 * second
        ).astype(bf16)
        return 0

    lax.fori_loop(0, width // WIDE, combine, 0)

    others = pl.ds(0, (n_dp - 1) * shard)
    pltpu.make_async_remote_copy(
        part.at[others], parts.at[others], p_send, p_recv, device_id=(partner, e), device_id_type=MESH
    ).wait_recv()
    pltpu.make_async_copy(part.at[owner_rows(dp)], parts.at[owner_rows(dp)], own_sem.at[4]).wait()

    def total(n, _):
        acc = None
        for p in range(n_dp):
            r = pl.ds(pl.multiple_of(p * shard + n * 32, 32), 32)
            term = parts[r, :].astype(f32)
            acc = term if acc is None else acc + term
        dgrad_ref[pl.ds(pl.multiple_of(n * 32, 32), 32), :] = acc.astype(bf16)
        return 0

    lax.fori_loop(0, shard // 32, total, 0)

    arrived(DX)
    to_rows(got.at[DX], rows_tmp, True)
    home = home0 + home1

    def collect(n, _):
        tgrad_ref[:, cols(n)] = jnp.dot(
            home, rows_tmp[:, cols(n)], preferred_element_type=f32
        ).astype(bf16)
        return 0

    lax.fori_loop(0, width // WIDE, collect, 0, unroll=True)

    for ph in range(4):
        drained(ph)
    for kind, src, full in stages:
        own3, on4 = pl.ds(0, 3 * shard), pl.ds(0, 4 * shard)
        pltpu.make_async_remote_copy(
            full.at[own3], full.at[own3], w_send.at[kind], w_recv.at[kind, dp],
            device_id=(partner, e), device_id_type=MESH,
        ).wait_send()
        pltpu.make_async_remote_copy(
            full.at[on4], full.at[on4], w_pass.at[kind], w_recv.at[kind, dp],
            device_id=(partner, e), device_id_type=MESH,
        ).wait_send()
    pltpu.make_async_remote_copy(
        part.at[others], parts.at[others], p_send, p_recv, device_id=(partner, e), device_id_type=MESH
    ).wait_send()


def put(*refs):
    n = len(refs) // 2
    copies = [pltpu.make_async_copy(refs[i], refs[n + i], refs[2 * n].at[i]) for i in range(n)]
    for copy in copies:
        copy.start()
    for copy in copies:
        copy.wait()


def put_out(*arrays):
    n = len(arrays)
    return pl.pallas_call(
        put,
        out_shape=[jax.ShapeDtypeStruct(a.shape, a.dtype) for a in arrays],
        in_specs=[pl.BlockSpec(memory_space=pltpu.VMEM)] * n,
        out_specs=[pl.BlockSpec(memory_space=pl.ANY)] * n,
        scratch_shapes=[pltpu.SemaphoreType.DMA((n,))],
        name="put_out",
    )(*[pltpu.with_memory_space_constraint(a, pltpu.VMEM) for a in arrays])


def per_device(tokens, out_grad, route_gates, route_slot, gate_weight, up_weight, down_weight):
    tok_dev, width = tokens.shape
    top = route_slot.shape[1]
    n_exp = lax.axis_size("expert")
    n_dp = lax.axis_size("dp")
    cap = max(2, (5 * tok_dev * top + 4 * n_exp - 1) // (4 * n_exp))
    rows = n_exp * cap
    ff = gate_weight.shape[2]
    shard = width // n_dp
    bf16, f32 = jnp.bfloat16, jnp.float32
    vmem = pl.BlockSpec(memory_space=pltpu.VMEM)
    away = pl.BlockSpec(memory_space=pl.ANY)
    dma = pltpu.SemaphoreType.DMA
    flat = rows * SUB
    moe, tgrad, dgrad = pl.pallas_call(
        functools.partial(layer, cap),
        out_shape=(
            pltpu.VMEM((tok_dev, width), bf16),
            pltpu.VMEM((tok_dev, width), bf16),
            pltpu.VMEM((shard, ff), bf16),
        ),
        in_specs=[vmem] * 4 + [away] * 3,
        out_specs=(vmem, vmem, vmem),
        scratch_shapes=[
            pltpu.VMEM((WIDE, WIDE), bf16),
            pltpu.VMEM((width, ff), bf16),
            pltpu.VMEM((width, ff), bf16),
            pltpu.VMEM((width, ff), bf16),
            pltpu.VMEM((4, flat, LANES), bf16),
            pltpu.VMEM((4, flat, LANES), bf16),
            pltpu.VMEM((rows, width), bf16),
            pltpu.VMEM((rows, width), bf16),
            pltpu.VMEM((rows, width), bf16),
            pltpu.VMEM((rows, ff), f32),
            pltpu.VMEM((rows, ff), f32),
            pltpu.VMEM((rows, ff), bf16),
            pltpu.VMEM((rows, ff), bf16),
            pltpu.VMEM((rows, ff), bf16),
            pltpu.VMEM((width, ff), bf16),
            pltpu.VMEM((width, ff), bf16),
            dma((4,)),
            dma((4,)),
            dma((5,)),
            dma((3,)),
            dma((3,)),
            dma((3,)),
            dma((3, n_dp)),
            dma,
            dma,
            pltpu.SemaphoreType.REGULAR((2,)),
        ],
        name="expert_layer",
        compiler_params=pltpu.CompilerParams(
            collective_id=0, has_side_effects=True, vmem_limit_bytes=60 * 1024 * 1024
        ),
    )(
        route_slot.T,
        route_gates.T,
        tokens,
        out_grad,
        gate_weight[0],
        up_weight[0],
        down_weight[0],
    )
    moe, tgrad, dgrad = put_out(moe, tgrad, dgrad)
    return moe, tgrad, dgrad[None]


def solution(mesh):
    rows = P(("dp", "expert"), None)
    weights = P("expert", "dp", None)
    return jax.shard_map(
        per_device,
        mesh=mesh,
        in_specs=(rows, rows, rows, rows, weights, weights, weights),
        out_specs=(rows, rows, weights),
        check_vma=False,
    )
```
